32 devices in a mesh: lat: 4 (over x, core), lon: 8 (over z, y).
Axes of the slice: x: 2, y: 2, z: 4, core: 2. Of those that a mesh axis runs over, the one named last changes fastest.
Arguments:
- fine_tokens: bfloat16 [2, 48, 96, 512], P(None, 'lat', 'lon'), may hold values from -6 to 6
- qkv_weight: bfloat16 [512, 1536], P(None, 'lat'), may hold values from -2 to 2
- proj_weight: bfloat16 [512, 512], P(None, 'lat'), may hold values from -0.25 to 0.25
- merge_one: bfloat16 [2048, 1024], P(None, 'lat'), may hold values from -0.125 to 0.125
- merge_two: bfloat16 [4096, 2048], P('lon'), may hold values from -0.09375 to 0.09375
- mlp_in: bfloat16 [2048, 8192], P(None, 'lon'), may hold values from -0.125 to 0.125
- mlp_out: bfloat16 [8192, 2048], P('lon'), may hold values from -0.125 to 0.125
- split_weight: bfloat16 [2048, 4096], P(None, 'lon'), may hold values from -0.125 to 0.125
Outputs:
- fine_out: float32 [2, 48, 96, 512], P(None, 'lat', 'lon')
- mid_out: float32 [2, 24, 48, 1024], P(None, 'lat', 'lon')
The draws below stay inside these ranges and needn't reach their ends.
All inputs are finite; a program needn't handle non-finite values.
Results may differ from the reference program's by a relative error of at most 0.029.
Values may be sent and summed in bfloat16 or wider, within the bound.
A program may use at most 64 MiB of HBM per device.

```python
import math
import jax
import jax.numpy as jnp
from jax import lax

D = 512
MID = 1024
TOP = 2048
EXPAND = 8192
HEADS = 8
LEV = 2
WIN_R = 6
WIN_C = 12
SHIFT_R = 3
SHIFT_C = 6
NR = 48
NC = 96
N_LON = 8


def draw_qkv_weight(key, part):
    values = jax.random.normal(key, (D, 3 * D), jnp.float32) / math.sqrt(D)
    return jnp.clip(values, -2.0, 2.0).astype(jnp.bfloat16)


def levels(key, extent, cuts, smallest, largest):
    gain, own = 1.0, jax.random.fold_in(key, 6)
    for dim, blocks in cuts:
        heights = jnp.exp(jax.random.uniform(jax.random.fold_in(own, dim), (blocks,), jnp.float32, smallest / len(cuts), largest / len(cuts)))
        gain = gain * jnp.repeat(heights, extent[dim] // blocks).reshape([-1 if axis == dim else 1 for axis in range(len(extent))])
    return gain


def normal_values(rng, dims, scale, most, split=(), held_as=jnp.bfloat16):
    drawn = jax.random.normal(rng, dims, jnp.float32) * scale
    if len(split) > 0:
        drawn = levels(rng, dims, split, -0.22, 0.18) * drawn
    return jnp.clip(drawn, min=-most, max=most).astype(held_as)


def setup_inputs(seed: int = 0) -> dict:
    streams_of = jax.random.split(jax.random.key(seed), 9)
    fine_tokens = normal_values(streams_of[0], (LEV, NR, NC, D), 1.0, 6.0, ((1, 4), (2, 8)))
    qkv_weight = draw_qkv_weight(jax.random.fold_in(streams_of[8], 71), 0)
    proj_weight = normal_values(streams_of[2], (D, D), D ** -0.5, 0.25, ((1, 4),))
    merge_one = normal_values(streams_of[3], (4 * D, MID), (4 * D) ** -0.5, 0.125, ((1, 4),))
    merge_two = normal_values(streams_of[4], (4 * MID, TOP), (4 * MID) ** -0.5, 0.09375, ((0, 8),))
    mlp_in = normal_values(streams_of[5], (TOP, EXPAND), TOP ** -0.5, 0.125, ((1, 8),))
    mlp_out = normal_values(streams_of[6], (EXPAND, TOP), (EXPAND // 4) ** -0.5, 0.125, ((0, 8),))
    split_weight = normal_values(streams_of[7], (TOP, 4 * MID), TOP ** -0.5, 0.125, ((1, 8),))
    return {"fine_tokens": fine_tokens, "qkv_weight": qkv_weight, "proj_weight": proj_weight, "merge_one": merge_one, "merge_two": merge_two, "mlp_in": mlp_in, "mlp_out": mlp_out, "split_weight": split_weight}


def layer_norm(values):
    centre = lax.optimization_barrier(jnp.mean(values, axis=-1, keepdims=True))
    shifted = values - centre
    spread = lax.optimization_barrier(jnp.mean(shifted * shifted, axis=-1, keepdims=True))
    return shifted * lax.rsqrt(spread + 1e-05)

def attend_group(qkv_group, row_index):
    wins = NC // WIN_C
    tokens = LEV * WIN_R * WIN_C
    head_dim = D // HEADS
    parts = qkv_group.reshape(LEV, WIN_R, wins, WIN_C, 3, HEADS, head_dim)
    parts = parts.transpose(2, 0, 1, 3, 4, 5, 6).reshape(wins, tokens, 3, HEADS, head_dim)
    query = parts[:, :, 0].astype(jnp.float32)
    keys = parts[:, :, 1].astype(jnp.float32)
    values = parts[:, :, 2].astype(jnp.float32)
    scores = jnp.einsum('wqhd,wkhd->whqk', query, keys) / math.sqrt(head_dim)
    wrapped = (row_index >= NR - SHIFT_R).astype(jnp.int32)
    labels = jnp.broadcast_to(wrapped[None, :, None], (LEV, WIN_R, WIN_C)).reshape(tokens)
    allowed = labels[:, None] == labels[None, :]
    scores = jnp.where(allowed[None, None], scores, jnp.float32(-1000000000.0))
    top = lax.optimization_barrier(jnp.max(scores, axis=-1, keepdims=True))
    expo = jnp.exp(scores - top)
    probs = (expo / lax.optimization_barrier(jnp.sum(expo, axis=-1, keepdims=True))).astype(jnp.bfloat16)
    heads_out = jnp.einsum('whqk,wkhd->wqhd', probs.astype(jnp.float32), values).astype(jnp.bfloat16)
    heads_out = heads_out.reshape(wins, LEV, WIN_R, WIN_C, D).transpose(1, 2, 0, 3, 4)
    return heads_out.reshape(LEV, WIN_R, NC, D)

def cat_four(grid):
    lev, rows, cols, width = grid.shape
    grid = grid.reshape(lev, rows // 2, 2, cols // 2, 2, width).transpose(0, 1, 3, 2, 4, 5)
    return grid.reshape(lev, rows // 2, cols // 2, 4 * width)

def reference(fine_tokens, qkv_weight, proj_weight, merge_one, merge_two, mlp_in, mlp_out, split_weight):
    moved = jnp.roll(fine_tokens, (-SHIFT_R, -SHIFT_C), axis=(1, 2))
    normed = layer_norm(moved.astype(jnp.float32)).astype(jnp.bfloat16).reshape(-1, D)
    qkv = jnp.dot(normed, qkv_weight, preferred_element_type=jnp.float32).astype(jnp.bfloat16)
    groups = NR // WIN_R
    qkv = qkv.reshape(LEV, groups, WIN_R, NC, 3 * D).transpose(1, 0, 2, 3, 4)
    row_ids = jnp.arange(NR, dtype=jnp.int32).reshape(groups, WIN_R)
    heads_out = lax.map(lambda pair: attend_group(pair[0], pair[1]), (qkv, row_ids))
    heads_out = heads_out.transpose(1, 0, 2, 3, 4).reshape(-1, D)
    attn = jnp.dot(heads_out, proj_weight, preferred_element_type=jnp.float32).astype(jnp.bfloat16)
    attn = attn.reshape(LEV, NR, NC, D)
    fine_out = fine_tokens.astype(jnp.float32) + jnp.roll(attn, (SHIFT_R, SHIFT_C), axis=(1, 2)).astype(jnp.float32)
    cat1 = layer_norm(cat_four(fine_out)).astype(jnp.bfloat16)
    merged1 = jnp.dot(cat1.reshape(-1, 4 * D), merge_one, preferred_element_type=jnp.float32).astype(jnp.bfloat16)
    merged1 = merged1.reshape(LEV, NR // 2, NC // 2, MID)
    normed2 = layer_norm(cat_four(merged1.astype(jnp.float32))).astype(jnp.bfloat16).reshape(-1, 4 * MID)
    count = normed2.shape[0]
    block = 4 * MID // N_LON

    def merge_step(index, total):
        piece = lax.dynamic_slice_in_dim(normed2, index * block, block, 1)
        rows = lax.dynamic_slice_in_dim(merge_two, index * block, block, 0)
        term = jnp.dot(piece, rows, preferred_element_type=jnp.float32).astype(jnp.bfloat16)
        return total + term.astype(jnp.float32)
    merged2 = lax.fori_loop(0, N_LON, merge_step, jnp.zeros((count, TOP), jnp.float32))
    normed3 = layer_norm(merged2).astype(jnp.bfloat16)
    hidden_block = EXPAND // N_LON

    def mlp_step(index, total):
        cols_in = lax.dynamic_slice_in_dim(mlp_in, index * hidden_block, hidden_block, 1)
        rows_out = lax.dynamic_slice_in_dim(mlp_out, index * hidden_block, hidden_block, 0)
        act = jax.nn.gelu(jnp.dot(normed3, cols_in, preferred_element_type=jnp.float32)).astype(jnp.bfloat16)
        term = jnp.dot(act, rows_out, preferred_element_type=jnp.float32).astype(jnp.bfloat16)
        return total + term.astype(jnp.float32)
    mlp = lax.fori_loop(0, N_LON, mlp_step, jnp.zeros((count, TOP), jnp.float32))
    coarse = (merged2 + mlp).astype(jnp.bfloat16)
    pieces = jnp.dot(coarse, split_weight, preferred_element_type=jnp.float32).astype(jnp.bfloat16)
    pieces = pieces.reshape(LEV, NR // 4, NC // 4, 2, 2, MID).transpose(0, 1, 3, 2, 4, 5)
    pieces = pieces.reshape(LEV, NR // 2, NC // 2, MID)
    mid_out = merged1.astype(jnp.float32) + pieces.astype(jnp.float32)
    return (fine_out, mid_out)
```

```python
import math

import jax
import jax.numpy as jnp
from jax import lax
from jax.experimental import pallas as pl
from jax.experimental.pallas import tpu as pltpu
from jax.sharding import PartitionSpec as P

MID = 1024
HEADS = 8
WIN_R = 6
WIN_C = 12
SHIFT_R = 3
SHIFT_C = 6


def from_behind(value, axis, steps):
    count = lax.axis_size(axis)
    pairs = [(source, (source + steps) % count) for source in range(count)]
    return lax.ppermute(value, axis, pairs)


def layer_norm(values):
    centre = jnp.mean(values, axis=-1, keepdims=True)
    shifted = values - centre
    spread = jnp.mean(shifted * shifted, axis=-1, keepdims=True)
    return shifted * lax.rsqrt(spread + 1e-05)


def cat_four(grid):
    lev, rows, cols, width = grid.shape
    grid = grid.reshape(lev, rows // 2, 2, cols // 2, 2, width).transpose(0, 1, 3, 2, 4, 5)
    return grid.reshape(lev * (rows // 2) * (cols // 2), 4 * width)


def coarse_kernel(
    blocks_ref, two_hbm, in_hbm, out_hbm, split_hbm, pieces_ref,
    two, w_in, w_out, split, landed, features, sent, summed, own, gathered, normed, act,
    sent2, summed2, gathered2, cols, sent3, landed3,
    load_sem, send_sem, recv_sem,
):
    count = lax.axis_size("lon")
    me = lax.axis_index("lon")
    own_count = blocks_ref.shape[1]
    width = own.shape[1]
    loads = [
        pltpu.make_async_copy(source, target, load_sem.at[index])
        for index, (source, target) in enumerate(
            ((two_hbm, two), (in_hbm, w_in), (out_hbm, w_out), (split_hbm, split))
        )
    ]
    for load in loads:
        load.start()
    barrier = pltpu.get_barrier_semaphore()

    def greet(step, carry):
        peer = lax.rem(me + step, count)
        pl.semaphore_signal(
            barrier, inc=1, device_id={"lon": peer}, device_id_type=pl.DeviceIdType.MESH
        )
        return carry

    lax.fori_loop(1, count, greet, 0)
    pl.semaphore_wait(barrier, count - 1)

    def copy_to(phase, peer, source, target):
        return pltpu.make_async_remote_copy(
            src_ref=source,
            dst_ref=target.at[me],
            send_sem=send_sem.at[phase, peer],
            recv_sem=recv_sem.at[phase, me],
            device_id={"lon": peer},
            device_id_type=pl.DeviceIdType.MESH,
        )

    def wait_from(phase, target):
        def body(step, carry):
            peer = lax.rem(me + step, count)
            pltpu.make_async_remote_copy(
                src_ref=target.at[peer],
                dst_ref=target.at[peer],
                send_sem=send_sem.at[phase, peer],
                recv_sem=recv_sem.at[phase, peer],
                device_id={"lon": peer},
                device_id_type=pl.DeviceIdType.MESH,
            ).wait_recv()
            return carry

        lax.fori_loop(1, count, body, 0)

    def wait_sent(phase, source_of, target):
        def body(step, carry):
            peer = lax.rem(me + step, count)
            copy_to(phase, peer, source_of(peer), target).wait_send()
            return carry

        lax.fori_loop(1, count, body, 0)

    def scatter_products(phase, left, weight, send, target):
        def product(peer):
            cut = pl.ds(pl.multiple_of(peer * width, width), width)
            return jnp.dot(left[...], weight[:, cut], preferred_element_type=jnp.float32)

        def body(step, carry):
            peer = lax.rem(me + step, count)
            send[peer] = product(peer).astype(jnp.bfloat16)
            copy_to(phase, peer, send.at[peer], target).start()
            return carry

        lax.fori_loop(1, count, body, 0)
        total = product(me)
        wait_from(phase, target)

        def add(step, total):
            return total + target[lax.rem(me + step, count)].astype(jnp.float32)

        return lax.fori_loop(1, count, add, total)

    def gather(phase, target):
        def body(step, carry):
            copy_to(phase, lax.rem(me + step, count), target.at[me], target).start()
            return carry

        lax.fori_loop(1, count, body, 0)
        wait_from(phase, target)

    def first(step, carry):
        peer = lax.rem(me + step, count)
        copy_to(0, peer, blocks_ref.at[peer], landed).start()
        return carry

    lax.fori_loop(1, count, first, 0)
    landed[me] = blocks_ref[me]
    wait_from(0, landed)
    for index in range(count):
        features[index * own_count : (index + 1) * own_count] = landed[index].astype(jnp.float32)
    normed[:, : features.shape[1]] = features[...].astype(jnp.bfloat16)
    loads[0].wait()
    merged = scatter_products(1, normed.at[:, : features.shape[1]], two, sent, summed)
    own[...] = merged
    gathered[me] = merged.astype(jnp.bfloat16)
    gather(2, gathered)

    total_width = count * width
    centre = gathered[0].astype(jnp.float32).sum(axis=-1, keepdims=True)
    for index in range(1, count):
        centre += gathered[index].astype(jnp.float32).sum(axis=-1, keepdims=True)
    centre = centre / total_width
    spread = jnp.zeros_like(centre)
    for index in range(count):
        shifted = gathered[index].astype(jnp.float32) - centre
        spread += (shifted * shifted).sum(axis=-1, keepdims=True)
    scale = lax.rsqrt(spread / total_width + 1e-05)
    for index in range(count):
        shifted = gathered[index].astype(jnp.float32) - centre
        normed[:, index * width : (index + 1) * width] = (shifted * scale).astype(jnp.bfloat16)
    loads[1].wait()

    tile = min(256, act.shape[1])

    def hidden(index, carry):
        cut = pl.ds(pl.multiple_of(index * tile, tile), tile)
        values = jnp.dot(normed[...], w_in[:, cut], preferred_element_type=jnp.float32)
        act[:, cut] = jax.nn.gelu(values).astype(jnp.bfloat16)
        return carry

    lax.fori_loop(0, act.shape[1] // tile, hidden, 0)
    loads[2].wait()
    mlp = scatter_products(3, act, w_out, sent2, summed2)
    gathered2[me] = (own[...] + mlp).astype(jnp.bfloat16)
    gather(4, gathered2)
    for index in range(count):
        normed[:, index * width : (index + 1) * width] = gathered2[index]
    loads[3].wait()
    cols[...] = jnp.dot(normed[...], split[...], preferred_element_type=jnp.float32)
    for index in range(count):
        sent3[index] = cols[index * own_count : (index + 1) * own_count].astype(jnp.bfloat16)

    def last(step, carry):
        peer = lax.rem(me + step, count)
        copy_to(5, peer, sent3.at[peer], landed3).start()
        return carry

    lax.fori_loop(1, count, last, 0)
    landed3[me] = sent3[me]
    wait_from(5, landed3)
    pieces_ref[...] = landed3[...]
    wait_sent(0, lambda peer: blocks_ref.at[peer], landed)
    wait_sent(1, lambda peer: sent.at[peer], summed)
    wait_sent(2, lambda peer: gathered.at[me], gathered)
    wait_sent(3, lambda peer: sent2.at[peer], summed2)
    wait_sent(4, lambda peer: gathered2.at[me], gathered2)
    wait_sent(5, lambda peer: sent3.at[peer], landed3)


def coarse_in_one(blocks, merge_two, mlp_in, mlp_out, split_weight):
    count, own_count, depth = blocks.shape
    tokens, top = count * own_count, merge_two.shape[1]
    width, hidden, split_width = top // count, mlp_in.shape[1], split_weight.shape[1]
    low = jnp.bfloat16
    whole = pl.BlockSpec(memory_space=pltpu.VMEM)
    apart = pl.BlockSpec(memory_space=pl.ANY)
    return pl.pallas_call(
        coarse_kernel,
        out_shape=jax.ShapeDtypeStruct((count, own_count, split_width), low),
        in_specs=[whole, apart, apart, apart, apart],
        out_specs=whole,
        scratch_shapes=[
            pltpu.VMEM(merge_two.shape, low),
            pltpu.VMEM(mlp_in.shape, low),
            pltpu.VMEM(mlp_out.shape, low),
            pltpu.VMEM(split_weight.shape, low),
            pltpu.VMEM((count, own_count, depth), low),
            pltpu.VMEM((tokens, depth), jnp.float32),
            pltpu.VMEM((count, tokens, width), low),
            pltpu.VMEM((count, tokens, width), low),
            pltpu.VMEM((tokens, width), jnp.float32),
            pltpu.VMEM((count, tokens, width), low),
            pltpu.VMEM((tokens, top), low),
            pltpu.VMEM((tokens, hidden), low),
            pltpu.VMEM((count, tokens, width), low),
            pltpu.VMEM((count, tokens, width), low),
            pltpu.VMEM((count, tokens, width), low),
            pltpu.VMEM((tokens, split_width), jnp.float32),
            pltpu.VMEM((count, own_count, split_width), low),
            pltpu.VMEM((count, own_count, split_width), low),
            pltpu.SemaphoreType.DMA((4,)),
            pltpu.SemaphoreType.DMA((6, count)),
            pltpu.SemaphoreType.DMA((6, count)),
        ],
        compiler_params=pltpu.CompilerParams(
            collective_id=0, has_side_effects=True, vmem_limit_bytes=40 * 1024 * 1024
        ),
    )(blocks, merge_two, mlp_in, mlp_out, split_weight)


def coarse_apart(normed2, merge_two, mlp_in, mlp_out, split_weight):
    own_count = normed2.shape[0]
    feature_parts = lax.all_to_all(normed2, "lon", split_axis=1, concat_axis=0, tiled=True)
    partial_value = jnp.dot(feature_parts, merge_two, preferred_element_type=jnp.float32)
    merged2 = lax.psum(partial_value.astype(jnp.bfloat16), "lon").astype(jnp.float32)
    normed3 = layer_norm(merged2).astype(jnp.bfloat16)
    act = jax.nn.gelu(jnp.dot(normed3, mlp_in, preferred_element_type=jnp.float32)).astype(
        jnp.bfloat16
    )
    mlp_own = lax.psum_scatter(
        jnp.dot(act, mlp_out, preferred_element_type=jnp.float32).astype(jnp.bfloat16),
        "lon",
        scatter_dimension=0,
        tiled=True,
    ).astype(jnp.float32)
    own_merged = lax.dynamic_slice_in_dim(merged2, lax.axis_index("lon") * own_count, own_count, 0)
    coarse = (own_merged + mlp_own).astype(jnp.bfloat16)
    split_cols = jnp.dot(
        lax.all_gather(coarse, "lon", axis=0, tiled=True),
        split_weight,
        preferred_element_type=jnp.float32,
    ).astype(jnp.bfloat16)
    return lax.all_to_all(split_cols, "lon", split_axis=0, concat_axis=1, tiled=True)


def on_device(
    fine_tokens, qkv_weight, proj_weight, merge_one, merge_two, mlp_in, mlp_out, split_weight
):
    levels, rows, cols, width = fine_tokens.shape
    lat_count = lax.axis_size("lat")
    head_dim = width // HEADS
    full_qkv, full_proj = (
        lax.all_gather(qkv_weight, "lat", axis=1, tiled=True),
        lax.all_gather(proj_weight, "lat", axis=1, tiled=True),
    )
    came = from_behind(fine_tokens[:, :, :SHIFT_C], "lon", -1)
    col_moved = jnp.concatenate([fine_tokens[:, :, SHIFT_C:], came], axis=2)
    came = from_behind(col_moved[:, :SHIFT_R], "lat", -1)
    moved = jnp.concatenate([col_moved[:, SHIFT_R:], came], axis=1)
    normed = layer_norm(moved.astype(jnp.float32)).astype(jnp.bfloat16).reshape(-1, width)
    qkv = jnp.dot(normed, full_qkv, preferred_element_type=jnp.float32).astype(jnp.bfloat16)
    row_wins = rows // WIN_R
    col_wins = cols // WIN_C
    wins = row_wins * col_wins
    tokens = levels * WIN_R * WIN_C
    parts = qkv.reshape(levels, row_wins, WIN_R, col_wins, WIN_C, 3, HEADS, head_dim)
    parts = parts.transpose(1, 3, 0, 2, 4, 5, 6, 7).reshape(wins, tokens, 3, HEADS, head_dim)
    scores = jnp.einsum(
        "wqhd,wkhd->whqk", parts[:, :, 0], parts[:, :, 1], preferred_element_type=jnp.float32
    )
    scores = scores / math.sqrt(head_dim)
    global_rows = lax.axis_index("lat") * rows + jnp.arange(rows, dtype=jnp.int32)
    wrapped = (global_rows >= rows * lat_count - SHIFT_R).astype(jnp.int32).reshape(row_wins, WIN_R)
    labels = jnp.broadcast_to(
        wrapped[:, None, None, :, None], (row_wins, col_wins, levels, WIN_R, WIN_C)
    )
    labels = labels.reshape(wins, tokens)
    allowed = labels[:, :, None] == labels[:, None, :]
    scores = jnp.where(allowed[:, None], scores, jnp.float32(-1000000000.0))
    top = jnp.max(scores, axis=-1, keepdims=True)
    expo = jnp.exp(scores - top)
    probs = (expo / jnp.sum(expo, axis=-1, keepdims=True)).astype(jnp.bfloat16)
    heads_out = jnp.einsum(
        "whqk,wkhd->wqhd", probs, parts[:, :, 2], preferred_element_type=jnp.float32
    )
    heads_out = heads_out.astype(jnp.bfloat16).reshape(
        row_wins, col_wins, levels, WIN_R, WIN_C, width
    )
    heads_out = heads_out.transpose(2, 0, 3, 1, 4, 5).reshape(-1, width)
    attn = jnp.dot(heads_out, full_proj, preferred_element_type=jnp.float32).astype(jnp.bfloat16)
    attn = attn.reshape(levels, rows, cols, width)
    came = from_behind(attn[:, rows - SHIFT_R :], "lat", 1)
    row_back = jnp.concatenate([came, attn[:, : rows - SHIFT_R]], axis=1)
    came = from_behind(row_back[:, :, cols - SHIFT_C :], "lon", 1)
    back = jnp.concatenate([came, row_back[:, :, : cols - SHIFT_C]], axis=2)
    fine_out = fine_tokens.astype(jnp.float32) + back.astype(jnp.float32)
    normed1 = layer_norm(cat_four(fine_out)).astype(jnp.bfloat16)
    merged1 = jnp.dot(
        normed1,
        lax.all_gather(merge_one, "lat", axis=1, tiled=True),
        preferred_element_type=jnp.float32,
    ).astype(jnp.bfloat16)
    merged1 = merged1.reshape(levels, rows // 2, cols // 2, MID)
    normed2 = layer_norm(cat_four(merged1.astype(jnp.float32))).astype(jnp.bfloat16)
    count = lax.axis_size("lon")
    if merge_two.shape[1] % (count * 128) == 0:
        blocks = normed2.reshape(normed2.shape[0], count, -1).transpose(1, 0, 2)
        pieces = coarse_in_one(blocks, merge_two, mlp_in, mlp_out, split_weight)
        pieces = pieces.transpose(1, 0, 2)
    else:
        pieces = coarse_apart(normed2, merge_two, mlp_in, mlp_out, split_weight)
    pieces = pieces.reshape(levels, rows // 4, cols // 4, 2, 2, MID).transpose(0, 1, 3, 2, 4, 5)
    pieces = pieces.reshape(levels, rows // 2, cols // 2, MID)
    mid_out = merged1.astype(jnp.float32) + pieces.astype(jnp.float32)
    return (fine_out, mid_out)


def solution(mesh):
    return jax.shard_map(
        on_device,
        mesh=mesh,
        in_specs=(
            P(None, "lat", "lon", None),
            P(None, "lat"),
            P(None, "lat"),
            P(None, "lat"),
            P("lon", None),
            P(None, "lon"),
            P("lon", None),
            P(None, "lon"),
        ),
        out_specs=(P(None, "lat", "lon", None), P(None, "lat", "lon", None)),
        check_vma=False,
    )
```

```python
import functools
import math

import jax
import jax.numpy as jnp
from jax import lax
from jax.experimental import pallas as pl
from jax.experimental.pallas import tpu as pltpu
from jax.sharding import PartitionSpec as P

MID = 1024
HEADS = 8
WIN_R = 6
WIN_C = 12
SHIFT_R = 3
SHIFT_C = 6


def layer_norm(values):
    centre = jnp.mean(values, axis=-1, keepdims=True)
    shifted = values - centre
    spread = jnp.mean(shifted * shifted, axis=-1, keepdims=True)
    return shifted * lax.rsqrt(spread + 1e-05)


def cat_four(grid):
    lev, rows, cols, width = grid.shape
    grid = grid.reshape(lev, rows // 2, 2, cols // 2, 2, width).transpose(0, 1, 3, 2, 4, 5)
    return grid.reshape(lev * (rows // 2) * (cols // 2), 4 * width)


def coarse_kernel(
    blocks_ref, two_hbm, in_hbm, out_hbm, split_hbm, pieces_ref,
    two, w_in, w_out, split, landed, features, sent, summed, own, gathered, normed, act,
    sent2, summed2, gathered2, cols, sent3, landed3,
    load_sem, send_sem, recv_sem,
):
    count = lax.axis_size("lon")
    me = lax.axis_index("lon")
    own_count = blocks_ref.shape[1]
    width = own.shape[1]
    loads = [
        pltpu.make_async_copy(source, target, load_sem.at[index])
        for index, (source, target) in enumerate(
            ((two_hbm, two), (in_hbm, w_in), (out_hbm, w_out), (split_hbm, split))
        )
    ]
    for load in loads:
        load.start()
    barrier = pltpu.get_barrier_semaphore()

    def greet(step, carry):
        peer = lax.rem(me + step, count)
        pl.semaphore_signal(
            barrier, inc=1, device_id={"lon": peer}, device_id_type=pl.DeviceIdType.MESH
        )
        return carry

    lax.fori_loop(1, count, greet, 0)
    pl.semaphore_wait(barrier, count - 1)

    def copy_to(phase, peer, source, target):
        return pltpu.make_async_remote_copy(
            src_ref=source,
            dst_ref=target.at[me],
            send_sem=send_sem.at[phase, peer],
            recv_sem=recv_sem.at[phase, me],
            device_id={"lon": peer},
            device_id_type=pl.DeviceIdType.MESH,
        )

    def wait_from(phase, target):
        def body(step, carry):
            peer = lax.rem(me + step, count)
            pltpu.make_async_remote_copy(
                src_ref=target.at[peer],
                dst_ref=target.at[peer],
                send_sem=send_sem.at[phase, peer],
                recv_sem=recv_sem.at[phase, peer],
                device_id={"lon": peer},
                device_id_type=pl.DeviceIdType.MESH,
            ).wait_recv()
            return carry

        lax.fori_loop(1, count, body, 0)

    def wait_sent(phase, source_of, target):
        def body(step, carry):
            peer = lax.rem(me + step, count)
            copy_to(phase, peer, source_of(peer), target).wait_send()
            return carry

        lax.fori_loop(1, count, body, 0)

    def scatter_products(phase, left, weight, send, target):
        def product(peer):
            cut = pl.ds(pl.multiple_of(peer * width, width), width)
            return jnp.dot(left[...], weight[:, cut], preferred_element_type=jnp.float32)

        def body(step, carry):
            peer = lax.rem(me + step, count)
            send[peer] = product(peer).astype(jnp.bfloat16)
            copy_to(phase, peer, send.at[peer], target).start()
            return carry

        lax.fori_loop(1, count, body, 0)
        total = product(me)
        wait_from(phase, target)

        def add(step, total):
            return total + target[lax.rem(me + step, count)].astype(jnp.float32)

        return lax.fori_loop(1, count, add, total)

    def gather(phase, target):
        def body(step, carry):
            copy_to(phase, lax.rem(me + step, count), target.at[me], target).start()
            return carry

        lax.fori_loop(1, count, body, 0)
        wait_from(phase, target)

    def first(step, carry):
        peer = lax.rem(me + step, count)
        copy_to(0, peer, blocks_ref.at[peer], landed).start()
        return carry

    lax.fori_loop(1, count, first, 0)
    landed[me] = blocks_ref[me]
    wait_from(0, landed)
    for index in range(count):
        features[index * own_count : (index + 1) * own_count] = landed[index].astype(jnp.float32)
    normed[:, : features.shape[1]] = features[...].astype(jnp.bfloat16)
    loads[0].wait()
    merged = scatter_products(1, normed.at[:, : features.shape[1]], two, sent, summed)
    own[...] = merged
    gathered[me] = merged.astype(jnp.bfloat16)
    gather(2, gathered)

    total_width = count * width
    centre = gathered[0].astype(jnp.float32).sum(axis=-1, keepdims=True)
    for index in range(1, count):
        centre += gathered[index].astype(jnp.float32).sum(axis=-1, keepdims=True)
    centre = centre / total_width
    spread = jnp.zeros_like(centre)
    for index in range(count):
        shifted = gathered[index].astype(jnp.float32) - centre
        spread += (shifted * shifted).sum(axis=-1, keepdims=True)
    scale = lax.rsqrt(spread / total_width + 1e-05)
    for index in range(count):
        shifted = gathered[index].astype(jnp.float32) - centre
        normed[:, index * width : (index + 1) * width] = (shifted * scale).astype(jnp.bfloat16)
    loads[1].wait()

    tile = min(256, act.shape[1])

    def hidden(index, carry):
        cut = pl.ds(pl.multiple_of(index * tile, tile), tile)
        values = jnp.dot(normed[...], w_in[:, cut], preferred_element_type=jnp.float32)
        act[:, cut] = jax.nn.gelu(values).astype(jnp.bfloat16)
        return carry

    lax.fori_loop(0, act.shape[1] // tile, hidden, 0)
    loads[2].wait()
    mlp = scatter_products(3, act, w_out, sent2, summed2)
    gathered2[me] = (own[...] + mlp).astype(jnp.bfloat16)
    gather(4, gathered2)
    for index in range(count):
        normed[:, index * width : (index + 1) * width] = gathered2[index]
    loads[3].wait()
    cols[...] = jnp.dot(normed[...], split[...], preferred_element_type=jnp.float32)
    for index in range(count):
        sent3[index] = cols[index * own_count : (index + 1) * own_count].astype(jnp.bfloat16)

    def last(step, carry):
        peer = lax.rem(me + step, count)
        copy_to(5, peer, sent3.at[peer], landed3).start()
        return carry

    lax.fori_loop(1, count, last, 0)
    landed3[me] = sent3[me]
    wait_from(5, landed3)
    pieces_ref[...] = landed3[...]
    wait_sent(0, lambda peer: blocks_ref.at[peer], landed)
    wait_sent(1, lambda peer: sent.at[peer], summed)
    wait_sent(2, lambda peer: gathered.at[me], gathered)
    wait_sent(3, lambda peer: sent2.at[peer], summed2)
    wait_sent(4, lambda peer: gathered2.at[me], gathered2)
    wait_sent(5, lambda peer: sent3.at[peer], landed3)


def coarse_in_one(blocks, merge_two, mlp_in, mlp_out, split_weight):
    count, own_count, depth = blocks.shape
    tokens, top = count * own_count, merge_two.shape[1]
    width, hidden, split_width = top // count, mlp_in.shape[1], split_weight.shape[1]
    low = jnp.bfloat16
    whole = pl.BlockSpec(memory_space=pltpu.VMEM)
    apart = pl.BlockSpec(memory_space=pl.ANY)
    return pl.pallas_call(
        coarse_kernel,
        out_shape=jax.ShapeDtypeStruct((count, own_count, split_width), low),
        in_specs=[whole, apart, apart, apart, apart],
        out_specs=whole,
        scratch_shapes=[
            pltpu.VMEM(merge_two.shape, low),
            pltpu.VMEM(mlp_in.shape, low),
            pltpu.VMEM(mlp_out.shape, low),
            pltpu.VMEM(split_weight.shape, low),
            pltpu.VMEM((count, own_count, depth), low),
            pltpu.VMEM((tokens, depth), jnp.float32),
            pltpu.VMEM((count, tokens, width), low),
            pltpu.VMEM((count, tokens, width), low),
            pltpu.VMEM((tokens, width), jnp.float32),
            pltpu.VMEM((count, tokens, width), low),
            pltpu.VMEM((tokens, top), low),
            pltpu.VMEM((tokens, hidden), low),
            pltpu.VMEM((count, tokens, width), low),
            pltpu.VMEM((count, tokens, width), low),
            pltpu.VMEM((count, tokens, width), low),
            pltpu.VMEM((tokens, split_width), jnp.float32),
            pltpu.VMEM((count, own_count, split_width), low),
            pltpu.VMEM((count, own_count, split_width), low),
            pltpu.SemaphoreType.DMA((4,)),
            pltpu.SemaphoreType.DMA((6, count)),
            pltpu.SemaphoreType.DMA((6, count)),
        ],
        compiler_params=pltpu.CompilerParams(
            collective_id=0, has_side_effects=True, vmem_limit_bytes=60 * 1024 * 1024
        ),
    )(blocks, merge_two, mlp_in, mlp_out, split_weight)


def coarse_apart(normed2, merge_two, mlp_in, mlp_out, split_weight):
    own_count = normed2.shape[0]
    feature_parts = lax.all_to_all(normed2, "lon", split_axis=1, concat_axis=0, tiled=True)
    partial_value = jnp.dot(feature_parts, merge_two, preferred_element_type=jnp.float32)
    merged2 = lax.psum(partial_value.astype(jnp.bfloat16), "lon").astype(jnp.float32)
    normed3 = layer_norm(merged2).astype(jnp.bfloat16)
    act = jax.nn.gelu(jnp.dot(normed3, mlp_in, preferred_element_type=jnp.float32)).astype(
        jnp.bfloat16
    )
    mlp_own = lax.psum_scatter(
        jnp.dot(act, mlp_out, preferred_element_type=jnp.float32).astype(jnp.bfloat16),
        "lon",
        scatter_dimension=0,
        tiled=True,
    ).astype(jnp.float32)
    own_merged = lax.dynamic_slice_in_dim(merged2, lax.axis_index("lon") * own_count, own_count, 0)
    coarse = (own_merged + mlp_own).astype(jnp.bfloat16)
    split_cols = jnp.dot(
        lax.all_gather(coarse, "lon", axis=0, tiled=True),
        split_weight,
        preferred_element_type=jnp.float32,
    ).astype(jnp.bfloat16)
    return lax.all_to_all(split_cols, "lon", split_axis=0, concat_axis=1, tiled=True)


def halo_kernel(direction, shards, *refs):
    edges, weights = refs[:3], refs[3 : 3 + shards]
    came, wholes = refs[3 + shards : 6 + shards], refs[6 + shards : 6 + 2 * shards]
    edge_send, edge_recv, own_sem, weight_send, weight_recv = refs[6 + 2 * shards :]
    lat_count, lon_count = lax.axis_size("lat"), lax.axis_size("lon")
    row, col = lax.axis_index("lat"), lax.axis_index("lon")
    mesh = pl.DeviceIdType.MESH

    def beside(sign):
        next_row = lax.rem(row + sign + lat_count, lat_count)
        next_col = lax.rem(col + sign + lon_count, lon_count)
        return (next_row, col), (row, next_col), (next_row, next_col)

    other_core = row + 1 - 2 * lax.rem(row, 2)
    other_chip = lax.rem(row + 2, 4)
    partners = beside(1) + beside(-1)
    if shards:
        partners += ((other_core, col), (other_chip, col))
    barrier = pltpu.get_barrier_semaphore()
    for partner in partners:
        pl.semaphore_signal(barrier, inc=1, device_id=partner, device_id_type=mesh)
    pl.semaphore_wait(barrier, len(partners))

    copies = []
    for index, target in enumerate(beside(direction)):
        copies.append(
            pltpu.make_async_remote_copy(
                src_ref=edges[index],
                dst_ref=came[index],
                send_sem=edge_send.at[index],
                recv_sem=edge_recv.at[index],
                device_id=target,
                device_id_type=mesh,
            )
        )
    for copy in copies:
        copy.start()

    def columns(index, owner):
        width = weights[index].shape[1]
        return wholes[index].at[:, pl.ds(pl.multiple_of(owner * width, width), width)]

    relays = []
    for index in range(shards):
        across = []
        for kind, target in enumerate((other_chip, other_core)):
            across.append(
                pltpu.make_async_remote_copy(
                    src_ref=weights[index],
                    dst_ref=columns(index, row),
                    send_sem=weight_send.at[index, kind],
                    recv_sem=weight_recv.at[index, kind],
                    device_id=(target, col),
                    device_id_type=mesh,
                )
            )
        for copy in across:
            copy.start()
        pltpu.make_async_copy(weights[index], columns(index, row), own_sem.at[index]).start()
        relays.append(across)
    for index in range(shards):
        relays[index][0].wait_recv()
        relay = pltpu.make_async_remote_copy(
            src_ref=columns(index, other_chip),
            dst_ref=columns(index, other_chip),
            send_sem=weight_send.at[index, 2],
            recv_sem=weight_recv.at[index, 2],
            device_id=(other_core, col),
            device_id_type=mesh,
        )
        relay.start()
        relays[index].append(relay)
    for index in range(shards):
        relays[index][0].wait_send()
        relays[index][1].wait()
        relays[index][2].wait()
        pltpu.make_async_copy(weights[index], columns(index, row), own_sem.at[index]).wait()
    for copy in copies:
        copy.wait()


def exchange(edges, direction, weights, identity):
    whole = pl.BlockSpec(memory_space=pltpu.VMEM)
    shards = len(weights)
    outs = [jax.ShapeDtypeStruct(edge.shape, edge.dtype) for edge in edges]
    outs += [
        jax.ShapeDtypeStruct((part.shape[0], 4 * part.shape[1]), part.dtype) for part in weights
    ]
    return pl.pallas_call(
        functools.partial(halo_kernel, direction, shards),
        out_shape=outs,
        in_specs=[whole] * (3 + shards),
        out_specs=[whole] * (3 + shards),
        scratch_shapes=[
            pltpu.SemaphoreType.DMA((3,)),
            pltpu.SemaphoreType.DMA((3,)),
            pltpu.SemaphoreType.DMA((max(shards, 1),)),
            pltpu.SemaphoreType.DMA((max(shards, 1), 3)),
            pltpu.SemaphoreType.DMA((max(shards, 1), 3)),
        ],
        compiler_params=pltpu.CompilerParams(collective_id=identity, has_side_effects=True),
    )(*edges, *weights)


def lat_swap(value, mask):
    return lax.ppermute(value, "lat", [(index, index ^ mask) for index in range(4)])


def in_owner_order(parts):
    index = lax.axis_index("lat")
    odd, high = index % 2 == 1, index >= 2
    a, b, c, d = parts
    a, b = jnp.where(odd, b, a), jnp.where(odd, a, b)
    c, d = jnp.where(odd, d, c), jnp.where(odd, c, d)
    a, c = jnp.where(high, c, a), jnp.where(high, a, c)
    b, d = jnp.where(high, d, b), jnp.where(high, b, d)
    return jnp.concatenate((a, b, c, d), axis=-1)


def on_device(
    fine_tokens, qkv_weight, proj_weight, merge_one, merge_two, mlp_in, mlp_out, split_weight
):
    levels, rows, cols, width = fine_tokens.shape
    lat_count = lax.axis_size("lat")
    head_dim = width // HEADS
    edges = (
        fine_tokens[:, :SHIFT_R, SHIFT_C:],
        fine_tokens[:, SHIFT_R:, :SHIFT_C],
        fine_tokens[:, :SHIFT_R, :SHIFT_C],
    )
    if lat_count == 4:
        row_came, col_came, both_came, full_qkv, full_proj = exchange(
            edges, -1, (qkv_weight, proj_weight), 1
        )
        merge_one, row_came = lax.optimization_barrier((merge_one, row_came))
        merge_far = lat_swap(merge_one, 2)
        merge_parts = (merge_one, lat_swap(merge_one, 1), merge_far, lat_swap(merge_far, 1))
    else:
        row_came, col_came, both_came = exchange(edges, -1, (), 1)
        full_qkv = lax.all_gather(qkv_weight, "lat", axis=1, tiled=True)
        full_proj = lax.all_gather(proj_weight, "lat", axis=1, tiled=True)
    upper = jnp.concatenate([fine_tokens[:, SHIFT_R:, SHIFT_C:], col_came], axis=2)
    lower = jnp.concatenate([row_came, both_came], axis=2)
    moved = jnp.concatenate([upper, lower], axis=1)
    normed = layer_norm(moved.astype(jnp.float32)).astype(jnp.bfloat16).reshape(-1, width)
    qkv = jnp.dot(normed, full_qkv, preferred_element_type=jnp.float32).astype(jnp.bfloat16)
    row_wins = rows // WIN_R
    col_wins = cols // WIN_C
    wins = row_wins * col_wins
    tokens = levels * WIN_R * WIN_C
    parts = qkv.reshape(levels, row_wins, WIN_R, col_wins, WIN_C, 3, HEADS, head_dim)
    parts = parts.transpose(1, 3, 0, 2, 4, 5, 6, 7).reshape(wins, tokens, 3, HEADS, head_dim)
    scores = jnp.einsum(
        "wqhd,wkhd->whqk", parts[:, :, 0], parts[:, :, 1], preferred_element_type=jnp.float32
    )
    scores = scores / math.sqrt(head_dim)
    global_rows = lax.axis_index("lat") * rows + jnp.arange(rows, dtype=jnp.int32)
    wrapped = (global_rows >= rows * lat_count - SHIFT_R).astype(jnp.int32).reshape(row_wins, WIN_R)
    labels = jnp.broadcast_to(
        wrapped[:, None, None, :, None], (row_wins, col_wins, levels, WIN_R, WIN_C)
    )
    labels = labels.reshape(wins, tokens)
    allowed = labels[:, :, None] == labels[:, None, :]
    scores = jnp.where(allowed[:, None], scores, jnp.float32(-1000000000.0))
    top = jnp.max(scores, axis=-1, keepdims=True)
    expo = jnp.exp(scores - top)
    probs = (expo / jnp.sum(expo, axis=-1, keepdims=True)).astype(jnp.bfloat16)
    heads_out = jnp.einsum(
        "whqk,wkhd->wqhd", probs, parts[:, :, 2], preferred_element_type=jnp.float32
    )
    heads_out = heads_out.astype(jnp.bfloat16).reshape(
        row_wins, col_wins, levels, WIN_R, WIN_C, width
    )
    heads_out = heads_out.transpose(2, 0, 3, 1, 4, 5).reshape(-1, width)
    attn = jnp.dot(heads_out, full_proj, preferred_element_type=jnp.float32).astype(jnp.bfloat16)
    attn = attn.reshape(levels, rows, cols, width)
    edges = (
        attn[:, rows - SHIFT_R :, : cols - SHIFT_C],
        attn[:, : rows - SHIFT_R, cols - SHIFT_C :],
        attn[:, rows - SHIFT_R :, cols - SHIFT_C :],
    )
    row_came, col_came, both_came = exchange(edges, 1, (), 2)
    upper = jnp.concatenate([both_came, row_came], axis=2)
    lower = jnp.concatenate([col_came, attn[:, : rows - SHIFT_R, : cols - SHIFT_C]], axis=2)
    back = jnp.concatenate([upper, lower], axis=1)
    fine_out = fine_tokens.astype(jnp.float32) + back.astype(jnp.float32)
    normed1 = layer_norm(cat_four(fine_out)).astype(jnp.bfloat16)
    if lat_count == 4:
        merged1 = in_owner_order(
            [
                jnp.dot(normed1, part, preferred_element_type=jnp.float32).astype(jnp.bfloat16)
                for part in merge_parts
            ]
        )
    else:
        merge_all = lax.all_gather(merge_one, "lat", axis=1, tiled=True)
        merged1 = jnp.dot(normed1, merge_all, preferred_element_type=jnp.float32)
        merged1 = merged1.astype(jnp.bfloat16)
    merged1 = merged1.reshape(levels, rows // 2, cols // 2, MID)
    normed2 = layer_norm(cat_four(merged1.astype(jnp.float32))).astype(jnp.bfloat16)
    count = lax.axis_size("lon")
    if merge_two.shape[1] % (count * 128) == 0:
        blocks = normed2.reshape(normed2.shape[0], count, -1).transpose(1, 0, 2)
        pieces = coarse_in_one(blocks, merge_two, mlp_in, mlp_out, split_weight)
        pieces = pieces.transpose(1, 0, 2)
    else:
        pieces = coarse_apart(normed2, merge_two, mlp_in, mlp_out, split_weight)
    pieces = pieces.reshape(levels, rows // 4, cols // 4, 2, 2, MID).transpose(0, 1, 3, 2, 4, 5)
    pieces = pieces.reshape(levels, rows // 2, cols // 2, MID)
    mid_out = merged1.astype(jnp.float32) + pieces.astype(jnp.float32)
    return (fine_out, mid_out)


def solution(mesh):
    return jax.shard_map(
        on_device,
        mesh=mesh,
        in_specs=(
            P(None, "lat", "lon", None),
            P(None, "lat"),
            P(None, "lat"),
            P(None, "lat"),
            P("lon", None),
            P(None, "lon"),
            P("lon", None),
            P(None, "lon"),
        ),
        out_specs=(P(None, "lat", "lon", None), P(None, "lat", "lon", None)),
        check_vma=False,
    )
```

```python
import functools
import math

import jax
import jax.numpy as jnp
from jax import lax
from jax.experimental import pallas as pl
from jax.experimental.pallas import tpu as pltpu
from jax.sharding import PartitionSpec as P

MID = 1024
HEADS = 8
WIN_R = 6
WIN_C = 12
SHIFT_R = 3
SHIFT_C = 6


def layer_norm(values):
    centre = jnp.mean(values, axis=-1, keepdims=True)
    shifted = values - centre
    spread = jnp.mean(shifted * shifted, axis=-1, keepdims=True)
    return shifted * lax.rsqrt(spread + 1e-05)


def cat_four(grid):
    lev, rows, cols, width = grid.shape
    grid = grid.reshape(lev, rows // 2, 2, cols // 2, 2, width).transpose(0, 1, 3, 2, 4, 5)
    return grid.reshape(lev * (rows // 2) * (cols // 2), 4 * width)


def coarse_kernel(
    blocks_ref, two_hbm, in_hbm, out_hbm, split_hbm, pieces_ref,
    two, w_in, w_out, split, landed, features, own, gathered, normed, act,
    gathered2, cols, sent3, landed3, total, partial_sent, partial_came,
    load_sem, send_sem, recv_sem, sum_send, sum_recv, relay_send, relay_recv,
):
    count = lax.axis_size("lon")
    me = lax.axis_index("lon")
    own_count = blocks_ref.shape[1]
    width = own.shape[1]
    loads = [
        pltpu.make_async_copy(source, target, load_sem.at[index])
        for index, (source, target) in enumerate(
            ((two_hbm, two), (in_hbm, w_in), (out_hbm, w_out), (split_hbm, split))
        )
    ]
    for load in loads:
        load.start()
    barrier = pltpu.get_barrier_semaphore()

    def greet(step, carry):
        peer = lax.rem(me + step, count)
        pl.semaphore_signal(
            barrier, inc=1, device_id={"lon": peer}, device_id_type=pl.DeviceIdType.MESH
        )
        return carry

    lax.fori_loop(1, count, greet, 0)
    pl.semaphore_wait(barrier, count - 1)

    def copy_to(phase, peer, source, target):
        return pltpu.make_async_remote_copy(
            src_ref=source,
            dst_ref=target.at[me],
            send_sem=send_sem.at[phase, peer],
            recv_sem=recv_sem.at[phase, me],
            device_id={"lon": peer},
            device_id_type=pl.DeviceIdType.MESH,
        )

    def wait_from(phase, target):
        def body(step, carry):
            peer = lax.rem(me + step, count)
            pltpu.make_async_remote_copy(
                src_ref=target.at[peer],
                dst_ref=target.at[peer],
                send_sem=send_sem.at[phase, peer],
                recv_sem=recv_sem.at[phase, peer],
                device_id={"lon": peer},
                device_id_type=pl.DeviceIdType.MESH,
            ).wait_recv()
            return carry

        lax.fori_loop(1, count, body, 0)

    def wait_sent(phase, source_of, target):
        def body(step, carry):
            peer = lax.rem(me + step, count)
            copy_to(phase, peer, source_of(peer), target).wait_send()
            return carry

        lax.fori_loop(1, count, body, 0)

    chips = count // 2
    z, y = me // 2, lax.rem(me, 2)
    partner = me + 1 - 2 * y
    up, down, over = 0, 1, 2

    def hop(source, target, sent_sem, came_sem, peer):
        return pltpu.make_async_remote_copy(
            src_ref=source,
            dst_ref=target,
            send_sem=sent_sem,
            recv_sem=came_sem,
            device_id={"lon": peer},
            device_id_type=pl.DeviceIdType.MESH,
        )

    def sum_hop(phase, kind, row, peer):
        return hop(
            partial_sent.at[phase, kind, row],
            partial_came.at[phase, kind, row],
            sum_send.at[phase, kind, row],
            sum_recv.at[phase, kind, row],
            peer,
        )

    def scatter_products(phase, left, weight):
        def product(peer):
            cut = pl.ds(pl.multiple_of(peer * width, width), width)
            return jnp.dot(left[...], weight[:, cut], preferred_element_type=jnp.float32)

        def across(row):
            partial_sent[phase, over, row] = product(2 * row + 1 - y).astype(jnp.bfloat16)
            sum_hop(phase, over, row, partner).start()

        def add(kind, row, peer):
            sum_hop(phase, kind, row, peer).wait_recv()
            total[...] += partial_came[phase, kind, row].astype(jnp.float32)

        def onward(kind, row, behind, source, peer):
            total[...] = product(2 * row + y)
            add(over, row, partner)

            @pl.when(behind)
            def _():
                add(kind, row, source)

            partial_sent[phase, kind, row] = total[...].astype(jnp.bfloat16)
            sum_hop(phase, kind, row, peer).start()

        for far in range(chips - 1, 0, -1):
            pl.when(z + far < chips)(lambda: across(z + far))
            pl.when(z - far >= 0)(lambda: across(z - far))
        across(z)
        for far in range(chips - 1, 0, -1):
            pl.when(z + far < chips)(lambda: onward(up, z + far, z > 0, me - 2, me + 2))
            pl.when(z - far >= 0)(lambda: onward(down, z - far, z < chips - 1, me + 2, me - 2))
        total[...] = product(me)
        add(over, z, partner)
        pl.when(z > 0)(lambda: add(up, z, me - 2))
        pl.when(z < chips - 1)(lambda: add(down, z, me + 2))
        return total[...]

    def wait_products(phase):
        for row in range(chips):
            sum_hop(phase, over, row, partner).wait_send()
        for far in range(1, chips):
            pl.when(z + far < chips)(lambda: sum_hop(phase, up, z + far, me + 2).wait_send())
            pl.when(z - far >= 0)(lambda: sum_hop(phase, down, z - far, me - 2).wait_send())

    def relay(phase, target, kind, block, peer):
        return hop(
            target.at[block],
            target.at[block],
            relay_send.at[phase, kind, block],
            relay_recv.at[phase, block],
            peer,
        )

    def relays(phase, target, act_on, arriving):
        pl.when(z < chips - 1)(lambda: act_on(relay(phase, target, up, me, me + 2)))
        pl.when(z > 0)(lambda: act_on(relay(phase, target, down, me, me - 2)))
        act_on(relay(phase, target, over, me, partner))
        for far in range(1, chips):

            @pl.when(z - far >= 0)
            def _():
                block = me - 2 * far
                if arriving:
                    relay(phase, target, up, block, me - 2).wait_recv()
                pl.when(z < chips - 1)(
                    lambda: act_on(relay(phase, target, up, block, me + 2))
                )
                act_on(relay(phase, target, over, block, partner))

            @pl.when(z + far < chips)
            def _():
                block = me + 2 * far
                if arriving:
                    relay(phase, target, down, block, me + 2).wait_recv()
                pl.when(z > 0)(lambda: act_on(relay(phase, target, down, block, me - 2)))
                act_on(relay(phase, target, over, block, partner))

    def gather(phase, target):
        relays(phase, target, lambda copy: copy.start(), True)
        for row in range(chips):
            relay(phase, target, over, 2 * row + 1 - y, partner).wait_recv()

    def wait_gather(phase, target):
        relays(phase, target, lambda copy: copy.wait_send(), False)

    def first(step, carry):
        peer = lax.rem(me + step, count)
        copy_to(0, peer, blocks_ref.at[peer], landed).start()
        return carry

    lax.fori_loop(1, count, first, 0)
    landed[me] = blocks_ref[me]
    wait_from(0, landed)
    for index in range(count):
        features[index * own_count : (index + 1) * own_count] = landed[index].astype(jnp.float32)
    normed[:, : features.shape[1]] = features[...].astype(jnp.bfloat16)
    loads[0].wait()
    merged = scatter_products(0, normed.at[:, : features.shape[1]], two)
    own[...] = merged
    gathered[me] = merged.astype(jnp.bfloat16)
    gather(0, gathered)

    total_width = count * width
    centre = gathered[0].astype(jnp.float32).sum(axis=-1, keepdims=True)
    for index in range(1, count):
        centre += gathered[index].astype(jnp.float32).sum(axis=-1, keepdims=True)
    centre = centre / total_width
    spread = jnp.zeros_like(centre)
    for index in range(count):
        shifted = gathered[index].astype(jnp.float32) - centre
        spread += (shifted * shifted).sum(axis=-1, keepdims=True)
    scale = lax.rsqrt(spread / total_width + 1e-05)
    for index in range(count):
        shifted = gathered[index].astype(jnp.float32) - centre
        normed[:, index * width : (index + 1) * width] = (shifted * scale).astype(jnp.bfloat16)
    loads[1].wait()

    tile = min(256, act.shape[1])

    def hidden(index, carry):
        cut = pl.ds(pl.multiple_of(index * tile, tile), tile)
        values = jnp.dot(normed[...], w_in[:, cut], preferred_element_type=jnp.float32)
        act[:, cut] = jax.nn.gelu(values).astype(jnp.bfloat16)
        return carry

    lax.fori_loop(0, act.shape[1] // tile, hidden, 0)
    loads[2].wait()
    mlp = scatter_products(1, act, w_out)
    gathered2[me] = (own[...] + mlp).astype(jnp.bfloat16)
    gather(1, gathered2)
    for index in range(count):
        normed[:, index * width : (index + 1) * width] = gathered2[index]
    loads[3].wait()
    cols[...] = jnp.dot(normed[...], split[...], preferred_element_type=jnp.float32)
    for index in range(count):
        sent3[index] = cols[index * own_count : (index + 1) * own_count].astype(jnp.bfloat16)

    def last(step, carry):
        peer = lax.rem(me + step, count)
        copy_to(1, peer, sent3.at[peer], landed3).start()
        return carry

    lax.fori_loop(1, count, last, 0)
    landed3[me] = sent3[me]
    wait_from(1, landed3)
    pieces_ref[...] = landed3[...]
    wait_sent(0, lambda peer: blocks_ref.at[peer], landed)
    wait_sent(1, lambda peer: sent3.at[peer], landed3)
    for phase, target in enumerate((gathered, gathered2)):
        wait_products(phase)
        wait_gather(phase, target)


def coarse_in_one(blocks, merge_two, mlp_in, mlp_out, split_weight):
    count, own_count, depth = blocks.shape
    tokens, top = count * own_count, merge_two.shape[1]
    width, hidden, split_width = top // count, mlp_in.shape[1], split_weight.shape[1]
    low = jnp.bfloat16
    whole = pl.BlockSpec(memory_space=pltpu.VMEM)
    apart = pl.BlockSpec(memory_space=pl.ANY)
    return pl.pallas_call(
        coarse_kernel,
        out_shape=jax.ShapeDtypeStruct((count, own_count, split_width), low),
        in_specs=[whole, apart, apart, apart, apart],
        out_specs=whole,
        scratch_shapes=[
            pltpu.VMEM(merge_two.shape, low),
            pltpu.VMEM(mlp_in.shape, low),
            pltpu.VMEM(mlp_out.shape, low),
            pltpu.VMEM(split_weight.shape, low),
            pltpu.VMEM((count, own_count, depth), low),
            pltpu.VMEM((tokens, depth), jnp.float32),
            pltpu.VMEM((tokens, width), jnp.float32),
            pltpu.VMEM((count, tokens, width), low),
            pltpu.VMEM((tokens, top), low),
            pltpu.VMEM((tokens, hidden), low),
            pltpu.VMEM((count, tokens, width), low),
            pltpu.VMEM((tokens, split_width), jnp.float32),
            pltpu.VMEM((count, own_count, split_width), low),
            pltpu.VMEM((count, own_count, split_width), low),
            pltpu.VMEM((tokens, width), jnp.float32),
            pltpu.VMEM((2, 3, count // 2, tokens, width), low),
            pltpu.VMEM((2, 3, count // 2, tokens, width), low),
            pltpu.SemaphoreType.DMA((4,)),
            pltpu.SemaphoreType.DMA((2, count)),
            pltpu.SemaphoreType.DMA((2, count)),
            pltpu.SemaphoreType.DMA((2, 3, count // 2)),
            pltpu.SemaphoreType.DMA((2, 3, count // 2)),
            pltpu.SemaphoreType.DMA((2, 3, count)),
            pltpu.SemaphoreType.DMA((2, count)),
        ],
        compiler_params=pltpu.CompilerParams(
            collective_id=0, has_side_effects=True, vmem_limit_bytes=60 * 1024 * 1024
        ),
    )(blocks, merge_two, mlp_in, mlp_out, split_weight)


def coarse_apart(normed2, merge_two, mlp_in, mlp_out, split_weight):
    own_count = normed2.shape[0]
    feature_parts = lax.all_to_all(normed2, "lon", split_axis=1, concat_axis=0, tiled=True)
    partial_value = jnp.dot(feature_parts, merge_two, preferred_element_type=jnp.float32)
    merged2 = lax.psum(partial_value.astype(jnp.bfloat16), "lon").astype(jnp.float32)
    normed3 = layer_norm(merged2).astype(jnp.bfloat16)
    act = jax.nn.gelu(jnp.dot(normed3, mlp_in, preferred_element_type=jnp.float32)).astype(
        jnp.bfloat16
    )
    mlp_own = lax.psum_scatter(
        jnp.dot(act, mlp_out, preferred_element_type=jnp.float32).astype(jnp.bfloat16),
        "lon",
        scatter_dimension=0,
        tiled=True,
    ).astype(jnp.float32)
    own_merged = lax.dynamic_slice_in_dim(merged2, lax.axis_index("lon") * own_count, own_count, 0)
    coarse = (own_merged + mlp_own).astype(jnp.bfloat16)
    split_cols = jnp.dot(
        lax.all_gather(coarse, "lon", axis=0, tiled=True),
        split_weight,
        preferred_element_type=jnp.float32,
    ).astype(jnp.bfloat16)
    return lax.all_to_all(split_cols, "lon", split_axis=0, concat_axis=1, tiled=True)


def halo_kernel(direction, shards, *refs):
    edges, weights = refs[:3], refs[3 : 3 + shards]
    came, wholes = refs[3 + shards : 6 + shards], refs[6 + shards : 6 + 2 * shards]
    edge_send, edge_recv, own_sem, weight_send, weight_recv = refs[6 + 2 * shards :]
    lat_count, lon_count = lax.axis_size("lat"), lax.axis_size("lon")
    row, col = lax.axis_index("lat"), lax.axis_index("lon")
    mesh = pl.DeviceIdType.MESH

    def beside(sign):
        next_row = lax.rem(row + sign + lat_count, lat_count)
        next_col = lax.rem(col + sign + lon_count, lon_count)
        return (next_row, col), (row, next_col), (next_row, next_col)

    other_core = row + 1 - 2 * lax.rem(row, 2)
    other_chip = lax.rem(row + 2, 4)
    partners = beside(1) + beside(-1)
    if shards:
        partners += ((other_core, col), (other_chip, col))
    barrier = pltpu.get_barrier_semaphore()
    for partner in partners:
        pl.semaphore_signal(barrier, inc=1, device_id=partner, device_id_type=mesh)
    pl.semaphore_wait(barrier, len(partners))

    copies = []
    for index, target in enumerate(beside(direction)):
        copies.append(
            pltpu.make_async_remote_copy(
                src_ref=edges[index],
                dst_ref=came[index],
                send_sem=edge_send.at[index],
                recv_sem=edge_recv.at[index],
                device_id=target,
                device_id_type=mesh,
            )
        )
    for copy in copies:
        copy.start()

    def columns(index, owner):
        width = weights[index].shape[1]
        return wholes[index].at[:, pl.ds(pl.multiple_of(owner * width, width), width)]

    relays = []
    for index in range(shards):
        across = []
        for kind, target in enumerate((other_chip, other_core)):
            across.append(
                pltpu.make_async_remote_copy(
                    src_ref=weights[index],
                    dst_ref=columns(index, row),
                    send_sem=weight_send.at[index, kind],
                    recv_sem=weight_recv.at[index, kind],
                    device_id=(target, col),
                    device_id_type=mesh,
                )
            )
        for copy in across:
            copy.start()
        pltpu.make_async_copy(weights[index], columns(index, row), own_sem.at[index]).start()
        relays.append(across)
    for index in range(shards):
        relays[index][0].wait_recv()
        relay = pltpu.make_async_remote_copy(
            src_ref=columns(index, other_chip),
            dst_ref=columns(index, other_chip),
            send_sem=weight_send.at[index, 2],
            recv_sem=weight_recv.at[index, 2],
            device_id=(other_core, col),
            device_id_type=mesh,
        )
        relay.start()
        relays[index].append(relay)
    for index in range(shards):
        relays[index][0].wait_send()
        relays[index][1].wait()
        relays[index][2].wait()
        pltpu.make_async_copy(weights[index], columns(index, row), own_sem.at[index]).wait()
    for copy in copies:
        copy.wait()


def exchange(edges, direction, weights, identity):
    whole = pl.BlockSpec(memory_space=pltpu.VMEM)
    shards = len(weights)
    outs = [jax.ShapeDtypeStruct(edge.shape, edge.dtype) for edge in edges]
    outs += [
        jax.ShapeDtypeStruct((part.shape[0], 4 * part.shape[1]), part.dtype) for part in weights
    ]
    return pl.pallas_call(
        functools.partial(halo_kernel, direction, shards),
        out_shape=outs,
        in_specs=[whole] * (3 + shards),
        out_specs=[whole] * (3 + shards),
        scratch_shapes=[
            pltpu.SemaphoreType.DMA((3,)),
            pltpu.SemaphoreType.DMA((3,)),
            pltpu.SemaphoreType.DMA((max(shards, 1),)),
            pltpu.SemaphoreType.DMA((max(shards, 1), 3)),
            pltpu.SemaphoreType.DMA((max(shards, 1), 3)),
        ],
        compiler_params=pltpu.CompilerParams(collective_id=identity, has_side_effects=True),
    )(*edges, *weights)


def lat_swap(value, mask):
    return lax.ppermute(value, "lat", [(index, index ^ mask) for index in range(4)])


def in_owner_order(parts):
    index = lax.axis_index("lat")
    odd, high = index % 2 == 1, index >= 2
    a, b, c, d = parts
    a, b = jnp.where(odd, b, a), jnp.where(odd, a, b)
    c, d = jnp.where(odd, d, c), jnp.where(odd, c, d)
    a, c = jnp.where(high, c, a), jnp.where(high, a, c)
    b, d = jnp.where(high, d, b), jnp.where(high, b, d)
    return jnp.concatenate((a, b, c, d), axis=-1)


def on_device(
    fine_tokens, qkv_weight, proj_weight, merge_one, merge_two, mlp_in, mlp_out, split_weight
):
    levels, rows, cols, width = fine_tokens.shape
    lat_count = lax.axis_size("lat")
    head_dim = width // HEADS
    edges = (
        fine_tokens[:, :SHIFT_R, SHIFT_C:],
        fine_tokens[:, SHIFT_R:, :SHIFT_C],
        fine_tokens[:, :SHIFT_R, :SHIFT_C],
    )
    if lat_count == 4:
        row_came, col_came, both_came, full_qkv, full_proj = exchange(
            edges, -1, (qkv_weight, proj_weight), 1
        )
        merge_one, row_came = lax.optimization_barrier((merge_one, row_came))
        merge_far = lat_swap(merge_one, 2)
        merge_parts = (merge_one, lat_swap(merge_one, 1), merge_far, lat_swap(merge_far, 1))
    else:
        row_came, col_came, both_came = exchange(edges, -1, (), 1)
        full_qkv = lax.all_gather(qkv_weight, "lat", axis=1, tiled=True)
        full_proj = lax.all_gather(proj_weight, "lat", axis=1, tiled=True)
    upper = jnp.concatenate([fine_tokens[:, SHIFT_R:, SHIFT_C:], col_came], axis=2)
    lower = jnp.concatenate([row_came, both_came], axis=2)
    moved = jnp.concatenate([upper, lower], axis=1)
    normed = layer_norm(moved.astype(jnp.float32)).astype(jnp.bfloat16).reshape(-1, width)
    qkv = jnp.dot(normed, full_qkv, preferred_element_type=jnp.float32).astype(jnp.bfloat16)
    row_wins = rows // WIN_R
    col_wins = cols // WIN_C
    wins = row_wins * col_wins
    tokens = levels * WIN_R * WIN_C
    parts = qkv.reshape(levels, row_wins, WIN_R, col_wins, WIN_C, 3, HEADS, head_dim)
    parts = parts.transpose(1, 3, 0, 2, 4, 5, 6, 7).reshape(wins, tokens, 3, HEADS, head_dim)
    scores = jnp.einsum(
        "wqhd,wkhd->whqk", parts[:, :, 0], parts[:, :, 1], preferred_element_type=jnp.float32
    )
    scores = scores / math.sqrt(head_dim)
    global_rows = lax.axis_index("lat") * rows + jnp.arange(rows, dtype=jnp.int32)
    wrapped = (global_rows >= rows * lat_count - SHIFT_R).astype(jnp.int32).reshape(row_wins, WIN_R)
    labels = jnp.broadcast_to(
        wrapped[:, None, None, :, None], (row_wins, col_wins, levels, WIN_R, WIN_C)
    )
    labels = labels.reshape(wins, tokens)
    allowed = labels[:, :, None] == labels[:, None, :]
    scores = jnp.where(allowed[:, None], scores, jnp.float32(-1000000000.0))
    top = jnp.max(scores, axis=-1, keepdims=True)
    expo = jnp.exp(scores - top)
    probs = (expo / jnp.sum(expo, axis=-1, keepdims=True)).astype(jnp.bfloat16)
    heads_out = jnp.einsum(
        "whqk,wkhd->wqhd", probs, parts[:, :, 2], preferred_element_type=jnp.float32
    )
    heads_out = heads_out.astype(jnp.bfloat16).reshape(
        row_wins, col_wins, levels, WIN_R, WIN_C, width
    )
    heads_out = heads_out.transpose(2, 0, 3, 1, 4, 5).reshape(-1, width)
    attn = jnp.dot(heads_out, full_proj, preferred_element_type=jnp.float32).astype(jnp.bfloat16)
    attn = attn.reshape(levels, rows, cols, width)
    edges = (
        attn[:, rows - SHIFT_R :, : cols - SHIFT_C],
        attn[:, : rows - SHIFT_R, cols - SHIFT_C :],
        attn[:, rows - SHIFT_R :, cols - SHIFT_C :],
    )
    row_came, col_came, both_came = exchange(edges, 1, (), 2)
    upper = jnp.concatenate([both_came, row_came], axis=2)
    lower = jnp.concatenate([col_came, attn[:, : rows - SHIFT_R, : cols - SHIFT_C]], axis=2)
    back = jnp.concatenate([upper, lower], axis=1)
    fine_out = fine_tokens.astype(jnp.float32) + back.astype(jnp.float32)
    normed1 = layer_norm(cat_four(fine_out)).astype(jnp.bfloat16)
    if lat_count == 4:
        merged1 = in_owner_order(
            [
                jnp.dot(normed1, part, preferred_element_type=jnp.float32).astype(jnp.bfloat16)
                for part in merge_parts
            ]
        )
    else:
        merge_all = lax.all_gather(merge_one, "lat", axis=1, tiled=True)
        merged1 = jnp.dot(normed1, merge_all, preferred_element_type=jnp.float32)
        merged1 = merged1.astype(jnp.bfloat16)
    merged1 = merged1.reshape(levels, rows // 2, cols // 2, MID)
    normed2 = layer_norm(cat_four(merged1.astype(jnp.float32))).astype(jnp.bfloat16)
    count = lax.axis_size("lon")
    if count % 2 == 0 and merge_two.shape[1] % (count * 128) == 0:
        blocks = normed2.reshape(normed2.shape[0], count, -1).transpose(1, 0, 2)
        pieces = coarse_in_one(blocks, merge_two, mlp_in, mlp_out, split_weight)
        pieces = pieces.transpose(1, 0, 2)
    else:
        pieces = coarse_apart(normed2, merge_two, mlp_in, mlp_out, split_weight)
    pieces = pieces.reshape(levels, rows // 4, cols // 4, 2, 2, MID).transpose(0, 1, 3, 2, 4, 5)
    pieces = pieces.reshape(levels, rows // 2, cols // 2, MID)
    mid_out = merged1.astype(jnp.float32) + pieces.astype(jnp.float32)
    return (fine_out, mid_out)


def solution(mesh):
    return jax.shard_map(
        on_device,
        mesh=mesh,
        in_specs=(
            P(None, "lat", "lon", None),
            P(None, "lat"),
            P(None, "lat"),
            P(None, "lat"),
            P("lon", None),
            P(None, "lon"),
            P("lon", None),
            P(None, "lon"),
        ),
        out_specs=(P(None, "lat", "lon", None), P(None, "lat", "lon", None)),
        check_vma=False,
    )
```

```python
import functools
import math

import jax
import jax.numpy as jnp
from jax import lax
from jax.experimental import pallas as pl
from jax.experimental.pallas import tpu as pltpu
from jax.sharding import PartitionSpec as P

MID = 1024
HEADS = 8
WIN_R = 6
WIN_C = 12
SHIFT_R = 3
SHIFT_C = 6


def layer_norm(values):
    centre = jnp.mean(values, axis=-1, keepdims=True)
    shifted = values - centre
    spread = jnp.mean(shifted * shifted, axis=-1, keepdims=True)
    return shifted * lax.rsqrt(spread + 1e-05)


def cat_four(grid):
    lev, rows, cols, width = grid.shape
    grid = grid.reshape(lev, rows // 2, 2, cols // 2, 2, width).transpose(0, 1, 3, 2, 4, 5)
    return grid.reshape(lev * (rows // 2) * (cols // 2), 4 * width)


def coarse_kernel(
    blocks_ref, two_hbm, in_hbm, out_hbm, split_hbm, pieces_ref,
    two, w_in, w_out, split, landed, features, sent, summed, own, gathered, normed, act,
    sent2, summed2, gathered2, cols, sent3, landed3,
    load_sem, send_sem, recv_sem,
):
    count = lax.axis_size("lon")
    me = lax.axis_index("lon")
    own_count = blocks_ref.shape[1]
    width = own.shape[1]
    loads = [
        pltpu.make_async_copy(source, target, load_sem.at[index])
        for index, (source, target) in enumerate(
            ((two_hbm, two), (in_hbm, w_in), (out_hbm, w_out), (split_hbm, split))
        )
    ]
    for load in loads:
        load.start()
    barrier = pltpu.get_barrier_semaphore()

    def greet(step, carry):
        peer = lax.rem(me + step, count)
        pl.semaphore_signal(
            barrier, inc=1, device_id={"lon": peer}, device_id_type=pl.DeviceIdType.MESH
        )
        return carry

    lax.fori_loop(1, count, greet, 0)
    pl.semaphore_wait(barrier, count - 1)

    def copy_to(phase, peer, source, target):
        return pltpu.make_async_remote_copy(
            src_ref=source,
            dst_ref=target.at[me],
            send_sem=send_sem.at[phase, peer],
            recv_sem=recv_sem.at[phase, me],
            device_id={"lon": peer},
            device_id_type=pl.DeviceIdType.MESH,
        )

    def wait_from(phase, target):
        def body(step, carry):
            peer = lax.rem(me + step, count)
            pltpu.make_async_remote_copy(
                src_ref=target.at[peer],
                dst_ref=target.at[peer],
                send_sem=send_sem.at[phase, peer],
                recv_sem=recv_sem.at[phase, peer],
                device_id={"lon": peer},
                device_id_type=pl.DeviceIdType.MESH,
            ).wait_recv()
            return carry

        lax.fori_loop(1, count, body, 0)

    def wait_sent(phase, source_of, target):
        def body(step, carry):
            peer = lax.rem(me + step, count)
            copy_to(phase, peer, source_of(peer), target).wait_send()
            return carry

        lax.fori_loop(1, count, body, 0)

    def scatter_products(phase, left, weight, send, target):
        def product(peer):
            cut = pl.ds(pl.multiple_of(peer * width, width), width)
            return jnp.dot(left[...], weight[:, cut], preferred_element_type=jnp.float32)

        def body(step, carry):
            peer = lax.rem(me + step, count)
            send[peer] = product(peer).astype(jnp.bfloat16)
            copy_to(phase, peer, send.at[peer], target).start()
            return carry

        lax.fori_loop(1, count, body, 0)
        total = product(me)
        wait_from(phase, target)

        def add(step, total):
            return total + target[lax.rem(me + step, count)].astype(jnp.float32)

        return lax.fori_loop(1, count, add, total)

    def gather(phase, target):
        def body(step, carry):
            copy_to(phase, lax.rem(me + step, count), target.at[me], target).start()
            return carry

        lax.fori_loop(1, count, body, 0)
        wait_from(phase, target)

    def first(step, carry):
        peer = lax.rem(me + step, count)
        copy_to(0, peer, blocks_ref.at[peer], landed).start()
        return carry

    lax.fori_loop(1, count, first, 0)
    landed[me] = blocks_ref[me]
    wait_from(0, landed)
    for index in range(count):
        features[index * own_count : (index + 1) * own_count] = landed[index].astype(jnp.float32)
    normed[:, : features.shape[1]] = features[...].astype(jnp.bfloat16)
    loads[0].wait()
    merged = scatter_products(1, normed.at[:, : features.shape[1]], two, sent, summed)
    own[...] = merged
    gathered[me] = merged.astype(jnp.bfloat16)
    gather(2, gathered)

    total_width = count * width
    centre = gathered[0].astype(jnp.float32).sum(axis=-1, keepdims=True)
    for index in range(1, count):
        centre += gathered[index].astype(jnp.float32).sum(axis=-1, keepdims=True)
    centre = centre / total_width
    spread = jnp.zeros_like(centre)
    for index in range(count):
        shifted = gathered[index].astype(jnp.float32) - centre
        spread += (shifted * shifted).sum(axis=-1, keepdims=True)
    scale = lax.rsqrt(spread / total_width + 1e-05)
    for index in range(count):
        shifted = gathered[index].astype(jnp.float32) - centre
        normed[:, index * width : (index + 1) * width] = (shifted * scale).astype(jnp.bfloat16)
    loads[1].wait()

    tile = min(256, act.shape[1])

    def hidden(index, carry):
        cut = pl.ds(pl.multiple_of(index * tile, tile), tile)
        values = jnp.dot(normed[...], w_in[:, cut], preferred_element_type=jnp.float32)
        act[:, cut] = jax.nn.gelu(values).astype(jnp.bfloat16)
        return carry

    lax.fori_loop(0, act.shape[1] // tile, hidden, 0)
    loads[2].wait()
    mlp = scatter_products(3, act, w_out, sent2, summed2)
    gathered2[me] = (own[...] + mlp).astype(jnp.bfloat16)
    gather(4, gathered2)
    for index in range(count):
        normed[:, index * width : (index + 1) * width] = gathered2[index]
    loads[3].wait()
    cols[...] = jnp.dot(normed[...], split[...], preferred_element_type=jnp.float32)
    for index in range(count):
        sent3[index] = cols[index * own_count : (index + 1) * own_count].astype(jnp.bfloat16)

    def last(step, carry):
        peer = lax.rem(me + step, count)
        copy_to(5, peer, sent3.at[peer], landed3).start()
        return carry

    lax.fori_loop(1, count, last, 0)
    landed3[me] = sent3[me]
    wait_from(5, landed3)
    pieces_ref[...] = landed3[...]
    wait_sent(0, lambda peer: blocks_ref.at[peer], landed)
    wait_sent(1, lambda peer: sent.at[peer], summed)
    wait_sent(2, lambda peer: gathered.at[me], gathered)
    wait_sent(3, lambda peer: sent2.at[peer], summed2)
    wait_sent(4, lambda peer: gathered2.at[me], gathered2)
    wait_sent(5, lambda peer: sent3.at[peer], landed3)


def coarse_in_one(blocks, merge_two, mlp_in, mlp_out, split_weight):
    count, own_count, depth = blocks.shape
    tokens, top = count * own_count, merge_two.shape[1]
    width, hidden, split_width = top // count, mlp_in.shape[1], split_weight.shape[1]
    low = jnp.bfloat16
    whole = pl.BlockSpec(memory_space=pltpu.VMEM)
    apart = pl.BlockSpec(memory_space=pl.ANY)
    return pl.pallas_call(
        coarse_kernel,
        out_shape=jax.ShapeDtypeStruct((count, own_count, split_width), low),
        in_specs=[whole, apart, apart, apart, apart],
        out_specs=whole,
        scratch_shapes=[
            pltpu.VMEM(merge_two.shape, low),
            pltpu.VMEM(mlp_in.shape, low),
            pltpu.VMEM(mlp_out.shape, low),
            pltpu.VMEM(split_weight.shape, low),
            pltpu.VMEM((count, own_count, depth), low),
            pltpu.VMEM((tokens, depth), jnp.float32),
            pltpu.VMEM((count, tokens, width), low),
            pltpu.VMEM((count, tokens, width), low),
            pltpu.VMEM((tokens, width), jnp.float32),
            pltpu.VMEM((count, tokens, width), low),
            pltpu.VMEM((tokens, top), low),
            pltpu.VMEM((tokens, hidden), low),
            pltpu.VMEM((count, tokens, width), low),
            pltpu.VMEM((count, tokens, width), low),
            pltpu.VMEM((count, tokens, width), low),
            pltpu.VMEM((tokens, split_width), jnp.float32),
            pltpu.VMEM((count, own_count, split_width), low),
            pltpu.VMEM((count, own_count, split_width), low),
            pltpu.SemaphoreType.DMA((4,)),
            pltpu.SemaphoreType.DMA((6, count)),
            pltpu.SemaphoreType.DMA((6, count)),
        ],
        compiler_params=pltpu.CompilerParams(
            collective_id=0, has_side_effects=True, vmem_limit_bytes=60 * 1024 * 1024
        ),
    )(blocks, merge_two, mlp_in, mlp_out, split_weight)


def coarse_apart(normed2, merge_two, mlp_in, mlp_out, split_weight):
    own_count = normed2.shape[0]
    feature_parts = lax.all_to_all(normed2, "lon", split_axis=1, concat_axis=0, tiled=True)
    partial_value = jnp.dot(feature_parts, merge_two, preferred_element_type=jnp.float32)
    merged2 = lax.psum(partial_value.astype(jnp.bfloat16), "lon").astype(jnp.float32)
    normed3 = layer_norm(merged2).astype(jnp.bfloat16)
    act = jax.nn.gelu(jnp.dot(normed3, mlp_in, preferred_element_type=jnp.float32)).astype(
        jnp.bfloat16
    )
    mlp_own = lax.psum_scatter(
        jnp.dot(act, mlp_out, preferred_element_type=jnp.float32).astype(jnp.bfloat16),
        "lon",
        scatter_dimension=0,
        tiled=True,
    ).astype(jnp.float32)
    own_merged = lax.dynamic_slice_in_dim(merged2, lax.axis_index("lon") * own_count, own_count, 0)
    coarse = (own_merged + mlp_own).astype(jnp.bfloat16)
    split_cols = jnp.dot(
        lax.all_gather(coarse, "lon", axis=0, tiled=True),
        split_weight,
        preferred_element_type=jnp.float32,
    ).astype(jnp.bfloat16)
    return lax.all_to_all(split_cols, "lon", split_axis=0, concat_axis=1, tiled=True)


def halo_kernel(direction, shards, *refs):
    edges, weights = refs[:3], refs[3 : 3 + shards]
    came, wholes = refs[3 + shards : 6 + shards], refs[6 + shards : 6 + 2 * shards]
    edge_send, edge_recv, own_sem, weight_send, weight_recv = refs[6 + 2 * shards :]
    lat_count, lon_count = lax.axis_size("lat"), lax.axis_size("lon")
    row, col = lax.axis_index("lat"), lax.axis_index("lon")
    mesh = pl.DeviceIdType.MESH

    def beside(sign):
        next_row = lax.rem(row + sign + lat_count, lat_count)
        next_col = lax.rem(col + sign + lon_count, lon_count)
        return (next_row, col), (row, next_col), (next_row, next_col)

    other_core = row + 1 - 2 * lax.rem(row, 2)
    other_chip = lax.rem(row + 2, 4)
    side = lax.rem(col, 2)
    pair = col + 1 - 2 * side
    partners = beside(1) + beside(-1)
    if shards:
        partners += ((other_core, col), (other_chip, col), (row, pair))
    barrier = pltpu.get_barrier_semaphore()
    for partner in partners:
        pl.semaphore_signal(barrier, inc=1, device_id=partner, device_id_type=mesh)
    pl.semaphore_wait(barrier, len(partners))

    copies = []
    for index, target in enumerate(beside(direction)):
        copies.append(
            pltpu.make_async_remote_copy(
                src_ref=edges[index],
                dst_ref=came[index],
                send_sem=edge_send.at[index],
                recv_sem=edge_recv.at[index],
                device_id=target,
                device_id_type=mesh,
            )
        )
    for copy in copies:
        copy.start()

    def columns(index, owner):
        width = weights[index].shape[1]
        return wholes[index].at[:, pl.ds(pl.multiple_of(owner * width, width), width)]

    def half(ref, index, which):
        depth = weights[index].shape[0] // 2
        return ref.at[pl.ds(pl.multiple_of(which * depth, depth), depth)]

    def send(index, kind, source, target, device):
        copy = pltpu.make_async_remote_copy(
            src_ref=source,
            dst_ref=target,
            send_sem=weight_send.at[index, kind],
            recv_sem=weight_recv.at[index, kind],
            device_id=device,
            device_id_type=mesh,
        )
        copy.start()
        return copy

    moves = []
    for index in range(shards):
        mine, held = weights[index], columns(index, row)
        away = send(
            index, 0, half(mine, index, side), half(held, index, side), (other_chip, col)
        )
        moves.append([away, send(index, 1, mine, held, (other_core, col))])
        pltpu.make_async_copy(mine, held, own_sem.at[index]).start()
    for index in range(shards):
        moves[index][0].wait_recv()
        part = half(columns(index, other_chip), index, side)
        moves[index].append(send(index, 2, part, part, (row, pair)))
        moves[index].append(send(index, 3, part, part, (other_core, col)))
    for index in range(shards):
        moves[index][2].wait_recv()
        part = half(columns(index, other_chip), index, 1 - side)
        moves[index].append(send(index, 4, part, part, (other_core, col)))
    for index in range(shards):
        away, core, paired, first, second = moves[index]
        for copy in (away, core, paired, first, second):
            copy.wait_send()
        for copy in (core, first, second):
            copy.wait_recv()
        pltpu.make_async_copy(weights[index], columns(index, row), own_sem.at[index]).wait()
    for copy in copies:
        copy.wait()


def exchange(edges, direction, weights, identity):
    whole = pl.BlockSpec(memory_space=pltpu.VMEM)
    shards = len(weights)
    outs = [jax.ShapeDtypeStruct(edge.shape, edge.dtype) for edge in edges]
    outs += [
        jax.ShapeDtypeStruct((part.shape[0], 4 * part.shape[1]), part.dtype) for part in weights
    ]
    return pl.pallas_call(
        functools.partial(halo_kernel, direction, shards),
        out_shape=outs,
        in_specs=[whole] * (3 + shards),
        out_specs=[whole] * (3 + shards),
        scratch_shapes=[
            pltpu.SemaphoreType.DMA((3,)),
            pltpu.SemaphoreType.DMA((3,)),
            pltpu.SemaphoreType.DMA((max(shards, 1),)),
            pltpu.SemaphoreType.DMA((max(shards, 1), 5)),
            pltpu.SemaphoreType.DMA((max(shards, 1), 5)),
        ],
        compiler_params=pltpu.CompilerParams(collective_id=identity, has_side_effects=True),
    )(*edges, *weights)


def lat_swap(value, mask):
    return lax.ppermute(value, "lat", [(index, index ^ mask) for index in range(4)])


def in_owner_order(parts):
    index = lax.axis_index("lat")
    odd, high = index % 2 == 1, index >= 2
    a, b, c, d = parts
    a, b = jnp.where(odd, b, a), jnp.where(odd, a, b)
    c, d = jnp.where(odd, d, c), jnp.where(odd, c, d)
    a, c = jnp.where(high, c, a), jnp.where(high, a, c)
    b, d = jnp.where(high, d, b), jnp.where(high, b, d)
    return jnp.concatenate((a, b, c, d), axis=-1)


def on_device(
    fine_tokens, qkv_weight, proj_weight, merge_one, merge_two, mlp_in, mlp_out, split_weight
):
    levels, rows, cols, width = fine_tokens.shape
    lat_count = lax.axis_size("lat")
    head_dim = width // HEADS
    edges = (
        fine_tokens[:, :SHIFT_R, SHIFT_C:],
        fine_tokens[:, SHIFT_R:, :SHIFT_C],
        fine_tokens[:, :SHIFT_R, :SHIFT_C],
    )
    if lat_count == 4 and lax.axis_size("lon") % 2 == 0:
        row_came, col_came, both_came, full_qkv, full_proj = exchange(
            edges, -1, (qkv_weight, proj_weight), 1
        )
        merge_one, row_came = lax.optimization_barrier((merge_one, row_came))
        merge_far = lat_swap(merge_one, 2)
        merge_parts = (merge_one, lat_swap(merge_one, 1), merge_far, lat_swap(merge_far, 1))
    else:
        row_came, col_came, both_came = exchange(edges, -1, (), 1)
        full_qkv = lax.all_gather(qkv_weight, "lat", axis=1, tiled=True)
        full_proj = lax.all_gather(proj_weight, "lat", axis=1, tiled=True)
    upper = jnp.concatenate([fine_tokens[:, SHIFT_R:, SHIFT_C:], col_came], axis=2)
    lower = jnp.concatenate([row_came, both_came], axis=2)
    moved = jnp.concatenate([upper, lower], axis=1)
    normed = layer_norm(moved.astype(jnp.float32)).astype(jnp.bfloat16).reshape(-1, width)
    qkv = jnp.dot(normed, full_qkv, preferred_element_type=jnp.float32).astype(jnp.bfloat16)
    row_wins = rows // WIN_R
    col_wins = cols // WIN_C
    wins = row_wins * col_wins
    tokens = levels * WIN_R * WIN_C
    parts = qkv.reshape(levels, row_wins, WIN_R, col_wins, WIN_C, 3, HEADS, head_dim)
    parts = parts.transpose(1, 3, 0, 2, 4, 5, 6, 7).reshape(wins, tokens, 3, HEADS, head_dim)
    scores = jnp.einsum(
        "wqhd,wkhd->whqk", parts[:, :, 0], parts[:, :, 1], preferred_element_type=jnp.float32
    )
    scores = scores / math.sqrt(head_dim)
    global_rows = lax.axis_index("lat") * rows + jnp.arange(rows, dtype=jnp.int32)
    wrapped = (global_rows >= rows * lat_count - SHIFT_R).astype(jnp.int32).reshape(row_wins, WIN_R)
    labels = jnp.broadcast_to(
        wrapped[:, None, None, :, None], (row_wins, col_wins, levels, WIN_R, WIN_C)
    )
    labels = labels.reshape(wins, tokens)
    allowed = labels[:, :, None] == labels[:, None, :]
    scores = jnp.where(allowed[:, None], scores, jnp.float32(-1000000000.0))
    top = jnp.max(scores, axis=-1, keepdims=True)
    expo = jnp.exp(scores - top)
    probs = (expo / jnp.sum(expo, axis=-1, keepdims=True)).astype(jnp.bfloat16)
    heads_out = jnp.einsum(
        "whqk,wkhd->wqhd", probs, parts[:, :, 2], preferred_element_type=jnp.float32
    )
    heads_out = heads_out.astype(jnp.bfloat16).reshape(
        row_wins, col_wins, levels, WIN_R, WIN_C, width
    )
    heads_out = heads_out.transpose(2, 0, 3, 1, 4, 5).reshape(-1, width)
    attn = jnp.dot(heads_out, full_proj, preferred_element_type=jnp.float32).astype(jnp.bfloat16)
    attn = attn.reshape(levels, rows, cols, width)
    edges = (
        attn[:, rows - SHIFT_R :, : cols - SHIFT_C],
        attn[:, : rows - SHIFT_R, cols - SHIFT_C :],
        attn[:, rows - SHIFT_R :, cols - SHIFT_C :],
    )
    row_came, col_came, both_came = exchange(edges, 1, (), 2)
    upper = jnp.concatenate([both_came, row_came], axis=2)
    lower = jnp.concatenate([col_came, attn[:, : rows - SHIFT_R, : cols - SHIFT_C]], axis=2)
    back = jnp.concatenate([upper, lower], axis=1)
    fine_out = fine_tokens.astype(jnp.float32) + back.astype(jnp.float32)
    normed1 = layer_norm(cat_four(fine_out)).astype(jnp.bfloat16)
    if lat_count == 4 and lax.axis_size("lon") % 2 == 0:
        merged1 = in_owner_order(
            [
                jnp.dot(normed1, part, preferred_element_type=jnp.float32).astype(jnp.bfloat16)
                for part in merge_parts
            ]
        )
    else:
        merge_all = lax.all_gather(merge_one, "lat", axis=1, tiled=True)
        merged1 = jnp.dot(normed1, merge_all, preferred_element_type=jnp.float32)
        merged1 = merged1.astype(jnp.bfloat16)
    merged1 = merged1.reshape(levels, rows // 2, cols // 2, MID)
    normed2 = layer_norm(cat_four(merged1.astype(jnp.float32))).astype(jnp.bfloat16)
    count = lax.axis_size("lon")
    if merge_two.shape[1] % (count * 128) == 0:
        blocks = normed2.reshape(normed2.shape[0], count, -1).transpose(1, 0, 2)
        pieces = coarse_in_one(blocks, merge_two, mlp_in, mlp_out, split_weight)
        pieces = pieces.transpose(1, 0, 2)
    else:
        pieces = coarse_apart(normed2, merge_two, mlp_in, mlp_out, split_weight)
    pieces = pieces.reshape(levels, rows // 4, cols // 4, 2, 2, MID).transpose(0, 1, 3, 2, 4, 5)
    pieces = pieces.reshape(levels, rows // 2, cols // 2, MID)
    mid_out = merged1.astype(jnp.float32) + pieces.astype(jnp.float32)
    return (fine_out, mid_out)


def solution(mesh):
    return jax.shard_map(
        on_device,
        mesh=mesh,
        in_specs=(
            P(None, "lat", "lon", None),
            P(None, "lat"),
            P(None, "lat"),
            P(None, "lat"),
            P("lon", None),
            P(None, "lon"),
            P("lon", None),
            P(None, "lon"),
        ),
        out_specs=(P(None, "lat", "lon", None), P(None, "lat", "lon", None)),
        check_vma=False,
    )
```

```python
import functools
import math

import jax
import jax.numpy as jnp
from jax import lax
from jax.experimental import pallas as pl
from jax.experimental.pallas import tpu as pltpu
from jax.sharding import PartitionSpec as P

MID = 1024
HEADS = 8
WIN_R = 6
WIN_C = 12
SHIFT_R = 3
SHIFT_C = 6


def layer_norm(values):
    centre = jnp.mean(values, axis=-1, keepdims=True)
    shifted = values - centre
    spread = jnp.mean(shifted * shifted, axis=-1, keepdims=True)
    return shifted * lax.rsqrt(spread + 1e-05)


def cat_four(grid):
    lev, rows, cols, width = grid.shape
    grid = grid.reshape(lev, rows // 2, 2, cols // 2, 2, width).transpose(0, 1, 3, 2, 4, 5)
    return grid.reshape(lev * (rows // 2) * (cols // 2), 4 * width)


def coarse_kernel(
    blocks_ref, two_hbm, in_hbm, out_hbm, split_hbm, pieces_ref,
    two, w_in, w_out, split, landed, features, sent, summed, own, gathered, normed, act,
    sent2, summed2, gathered2, cols, sent3, landed3,
    load_sem, send_sem, recv_sem, relay_send, relay_recv,
):
    count = lax.axis_size("lon")
    me = lax.axis_index("lon")
    own_count = blocks_ref.shape[1]
    width = own.shape[1]
    loads = [
        pltpu.make_async_copy(source, target, load_sem.at[index])
        for index, (source, target) in enumerate(
            ((two_hbm, two), (in_hbm, w_in), (out_hbm, w_out), (split_hbm, split))
        )
    ]
    for load in loads:
        load.start()
    barrier = pltpu.get_barrier_semaphore()

    def greet(step, carry):
        peer = lax.rem(me + step, count)
        pl.semaphore_signal(
            barrier, inc=1, device_id={"lon": peer}, device_id_type=pl.DeviceIdType.MESH
        )
        return carry

    lax.fori_loop(1, count, greet, 0)
    pl.semaphore_wait(barrier, count - 1)

    def copy_to(phase, peer, source, target):
        return pltpu.make_async_remote_copy(
            src_ref=source,
            dst_ref=target.at[me],
            send_sem=send_sem.at[phase, peer],
            recv_sem=recv_sem.at[phase, me],
            device_id={"lon": peer},
            device_id_type=pl.DeviceIdType.MESH,
        )

    def wait_from(phase, target):
        def body(step, carry):
            peer = lax.rem(me + step, count)
            pltpu.make_async_remote_copy(
                src_ref=target.at[peer],
                dst_ref=target.at[peer],
                send_sem=send_sem.at[phase, peer],
                recv_sem=recv_sem.at[phase, peer],
                device_id={"lon": peer},
                device_id_type=pl.DeviceIdType.MESH,
            ).wait_recv()
            return carry

        lax.fori_loop(1, count, body, 0)

    def wait_sent(phase, source_of, target):
        def body(step, carry):
            peer = lax.rem(me + step, count)
            copy_to(phase, peer, source_of(peer), target).wait_send()
            return carry

        lax.fori_loop(1, count, body, 0)

    def scatter_products(phase, left, weight, send, target):
        def product(peer):
            cut = pl.ds(pl.multiple_of(peer * width, width), width)
            return jnp.dot(left[...], weight[:, cut], preferred_element_type=jnp.float32)

        def body(step, carry):
            peer = lax.rem(me + step, count)
            send[peer] = product(peer).astype(jnp.bfloat16)
            copy_to(phase, peer, send.at[peer], target).start()
            return carry

        lax.fori_loop(1, count, body, 0)
        total = product(me)
        wait_from(phase, target)

        def add(step, total):
            return total + target[lax.rem(me + step, count)].astype(jnp.float32)

        return lax.fori_loop(1, count, add, total)

    chips = count // 2
    z, y = me // 2, lax.rem(me, 2)
    partner = me + 1 - 2 * y
    up, down, over = 0, 1, 2

    def hop(source, target, sent_sem, came_sem, peer):
        return pltpu.make_async_remote_copy(
            src_ref=source,
            dst_ref=target,
            send_sem=sent_sem,
            recv_sem=came_sem,
            device_id={"lon": peer},
            device_id_type=pl.DeviceIdType.MESH,
        )

    def relay(phase, target, kind, block, peer):
        return hop(
            target.at[block],
            target.at[block],
            relay_send.at[phase, kind, block],
            relay_recv.at[phase, block],
            peer,
        )

    def relays(phase, target, act_on, arriving):
        pl.when(z < chips - 1)(lambda: act_on(relay(phase, target, up, me, me + 2)))
        pl.when(z > 0)(lambda: act_on(relay(phase, target, down, me, me - 2)))
        act_on(relay(phase, target, over, me, partner))
        for far in range(1, chips):

            @pl.when(z - far >= 0)
            def _():
                block = me - 2 * far
                if arriving:
                    relay(phase, target, up, block, me - 2).wait_recv()
                pl.when(z < chips - 1)(
                    lambda: act_on(relay(phase, target, up, block, me + 2))
                )
                act_on(relay(phase, target, over, block, partner))

            @pl.when(z + far < chips)
            def _():
                block = me + 2 * far
                if arriving:
                    relay(phase, target, down, block, me + 2).wait_recv()
                pl.when(z > 0)(lambda: act_on(relay(phase, target, down, block, me - 2)))
                act_on(relay(phase, target, over, block, partner))

    def gather(phase, target):
        relays(phase, target, lambda copy: copy.start(), True)
        for row in range(chips):
            relay(phase, target, over, 2 * row + 1 - y, partner).wait_recv()

    def wait_gather(phase, target):
        relays(phase, target, lambda copy: copy.wait_send(), False)

    def first(step, carry):
        peer = lax.rem(me + step, count)
        copy_to(0, peer, blocks_ref.at[peer], landed).start()
        return carry

    lax.fori_loop(1, count, first, 0)
    landed[me] = blocks_ref[me]
    wait_from(0, landed)
    for index in range(count):
        features[index * own_count : (index + 1) * own_count] = landed[index].astype(jnp.float32)
    normed[:, : features.shape[1]] = features[...].astype(jnp.bfloat16)
    loads[0].wait()
    merged = scatter_products(1, normed.at[:, : features.shape[1]], two, sent, summed)
    own[...] = merged
    gathered[me] = merged.astype(jnp.bfloat16)
    gather(0, gathered)

    total_width = count * width
    centre = gathered[0].astype(jnp.float32).sum(axis=-1, keepdims=True)
    for index in range(1, count):
        centre += gathered[index].astype(jnp.float32).sum(axis=-1, keepdims=True)
    centre = centre / total_width
    spread = jnp.zeros_like(centre)
    for index in range(count):
        shifted = gathered[index].astype(jnp.float32) - centre
        spread += (shifted * shifted).sum(axis=-1, keepdims=True)
    scale = lax.rsqrt(spread / total_width + 1e-05)
    for index in range(count):
        shifted = gathered[index].astype(jnp.float32) - centre
        normed[:, index * width : (index + 1) * width] = (shifted * scale).astype(jnp.bfloat16)
    loads[1].wait()

    tile = min(256, act.shape[1])

    def hidden(index, carry):
        cut = pl.ds(pl.multiple_of(index * tile, tile), tile)
        values = jnp.dot(normed[...], w_in[:, cut], preferred_element_type=jnp.float32)
        act[:, cut] = jax.nn.gelu(values).astype(jnp.bfloat16)
        return carry

    lax.fori_loop(0, act.shape[1] // tile, hidden, 0)
    loads[2].wait()
    mlp = scatter_products(3, act, w_out, sent2, summed2)
    gathered2[me] = (own[...] + mlp).astype(jnp.bfloat16)
    gather(1, gathered2)
    for index in range(count):
        normed[:, index * width : (index + 1) * width] = gathered2[index]
    loads[3].wait()
    cols[...] = jnp.dot(normed[...], split[...], preferred_element_type=jnp.float32)
    for index in range(count):
        sent3[index] = cols[index * own_count : (index + 1) * own_count].astype(jnp.bfloat16)

    def last(step, carry):
        peer = lax.rem(me + step, count)
        copy_to(5, peer, sent3.at[peer], landed3).start()
        return carry

    lax.fori_loop(1, count, last, 0)
    landed3[me] = sent3[me]
    wait_from(5, landed3)
    pieces_ref[...] = landed3[...]
    wait_sent(0, lambda peer: blocks_ref.at[peer], landed)
    wait_sent(1, lambda peer: sent.at[peer], summed)
    wait_gather(0, gathered)
    wait_sent(3, lambda peer: sent2.at[peer], summed2)
    wait_gather(1, gathered2)
    wait_sent(5, lambda peer: sent3.at[peer], landed3)


def coarse_in_one(blocks, merge_two, mlp_in, mlp_out, split_weight):
    count, own_count, depth = blocks.shape
    tokens, top = count * own_count, merge_two.shape[1]
    width, hidden, split_width = top // count, mlp_in.shape[1], split_weight.shape[1]
    low = jnp.bfloat16
    whole = pl.BlockSpec(memory_space=pltpu.VMEM)
    apart = pl.BlockSpec(memory_space=pl.ANY)
    return pl.pallas_call(
        coarse_kernel,
        out_shape=jax.ShapeDtypeStruct((count, own_count, split_width), low),
        in_specs=[whole, apart, apart, apart, apart],
        out_specs=whole,
        scratch_shapes=[
            pltpu.VMEM(merge_two.shape, low),
            pltpu.VMEM(mlp_in.shape, low),
            pltpu.VMEM(mlp_out.shape, low),
            pltpu.VMEM(split_weight.shape, low),
            pltpu.VMEM((count, own_count, depth), low),
            pltpu.VMEM((tokens, depth), jnp.float32),
            pltpu.VMEM((count, tokens, width), low),
            pltpu.VMEM((count, tokens, width), low),
            pltpu.VMEM((tokens, width), jnp.float32),
            pltpu.VMEM((count, tokens, width), low),
            pltpu.VMEM((tokens, top), low),
            pltpu.VMEM((tokens, hidden), low),
            pltpu.VMEM((count, tokens, width), low),
            pltpu.VMEM((count, tokens, width), low),
            pltpu.VMEM((count, tokens, width), low),
            pltpu.VMEM((tokens, split_width), jnp.float32),
            pltpu.VMEM((count, own_count, split_width), low),
            pltpu.VMEM((count, own_count, split_width), low),
            pltpu.SemaphoreType.DMA((4,)),
            pltpu.SemaphoreType.DMA((6, count)),
            pltpu.SemaphoreType.DMA((6, count)),
            pltpu.SemaphoreType.DMA((2, 3, count)),
            pltpu.SemaphoreType.DMA((2, count)),
        ],
        compiler_params=pltpu.CompilerParams(
            collective_id=0, has_side_effects=True, vmem_limit_bytes=60 * 1024 * 1024
        ),
    )(blocks, merge_two, mlp_in, mlp_out, split_weight)


def coarse_apart(normed2, merge_two, mlp_in, mlp_out, split_weight):
    own_count = normed2.shape[0]
    feature_parts = lax.all_to_all(normed2, "lon", split_axis=1, concat_axis=0, tiled=True)
    partial_value = jnp.dot(feature_parts, merge_two, preferred_element_type=jnp.float32)
    merged2 = lax.psum(partial_value.astype(jnp.bfloat16), "lon").astype(jnp.float32)
    normed3 = layer_norm(merged2).astype(jnp.bfloat16)
    act = jax.nn.gelu(jnp.dot(normed3, mlp_in, preferred_element_type=jnp.float32)).astype(
        jnp.bfloat16
    )
    mlp_own = lax.psum_scatter(
        jnp.dot(act, mlp_out, preferred_element_type=jnp.float32).astype(jnp.bfloat16),
        "lon",
        scatter_dimension=0,
        tiled=True,
    ).astype(jnp.float32)
    own_merged = lax.dynamic_slice_in_dim(merged2, lax.axis_index("lon") * own_count, own_count, 0)
    coarse = (own_merged + mlp_own).astype(jnp.bfloat16)
    split_cols = jnp.dot(
        lax.all_gather(coarse, "lon", axis=0, tiled=True),
        split_weight,
        preferred_element_type=jnp.float32,
    ).astype(jnp.bfloat16)
    return lax.all_to_all(split_cols, "lon", split_axis=0, concat_axis=1, tiled=True)


def halo_kernel(direction, shards, *refs):
    edges, weights = refs[:3], refs[3 : 3 + shards]
    came, wholes = refs[3 + shards : 6 + shards], refs[6 + shards : 6 + 2 * shards]
    edge_send, edge_recv, own_sem, weight_send, weight_recv = refs[6 + 2 * shards :]
    lat_count, lon_count = lax.axis_size("lat"), lax.axis_size("lon")
    row, col = lax.axis_index("lat"), lax.axis_index("lon")
    mesh = pl.DeviceIdType.MESH

    def beside(sign):
        next_row = lax.rem(row + sign + lat_count, lat_count)
        next_col = lax.rem(col + sign + lon_count, lon_count)
        return (next_row, col), (row, next_col), (next_row, next_col)

    other_core = row + 1 - 2 * lax.rem(row, 2)
    other_chip = lax.rem(row + 2, 4)
    side = lax.rem(col, 2)
    pair = col + 1 - 2 * side
    partners = beside(1) + beside(-1)
    if shards:
        partners += ((other_core, col), (other_chip, col), (row, pair))
    barrier = pltpu.get_barrier_semaphore()
    for partner in partners:
        pl.semaphore_signal(barrier, inc=1, device_id=partner, device_id_type=mesh)
    pl.semaphore_wait(barrier, len(partners))

    copies = []
    for index, target in enumerate(beside(direction)):
        copies.append(
            pltpu.make_async_remote_copy(
                src_ref=edges[index],
                dst_ref=came[index],
                send_sem=edge_send.at[index],
                recv_sem=edge_recv.at[index],
                device_id=target,
                device_id_type=mesh,
            )
        )
    for copy in copies:
        copy.start()

    def columns(index, owner):
        width = weights[index].shape[1]
        return wholes[index].at[:, pl.ds(pl.multiple_of(owner * width, width), width)]

    def half(ref, index, which):
        depth = weights[index].shape[0] // 2
        return ref.at[pl.ds(pl.multiple_of(which * depth, depth), depth)]

    def send(index, kind, source, target, device):
        copy = pltpu.make_async_remote_copy(
            src_ref=source,
            dst_ref=target,
            send_sem=weight_send.at[index, kind],
            recv_sem=weight_recv.at[index, kind],
            device_id=device,
            device_id_type=mesh,
        )
        copy.start()
        return copy

    moves = []
    for index in range(shards):
        mine, held = weights[index], columns(index, row)
        away = send(
            index, 0, half(mine, index, side), half(held, index, side), (other_chip, col)
        )
        moves.append([away, send(index, 1, mine, held, (other_core, col))])
        pltpu.make_async_copy(mine, held, own_sem.at[index]).start()
    for index in range(shards):
        moves[index][0].wait_recv()
        part = half(columns(index, other_chip), index, side)
        moves[index].append(send(index, 2, part, part, (row, pair)))
        moves[index].append(send(index, 3, part, part, (other_core, col)))
    for index in range(shards):
        moves[index][2].wait_recv()
        part = half(columns(index, other_chip), index, 1 - side)
        moves[index].append(send(index, 4, part, part, (other_core, col)))
    for index in range(shards):
        away, core, paired, first, second = moves[index]
        for copy in (away, core, paired, first, second):
            copy.wait_send()
        for copy in (core, first, second):
            copy.wait_recv()
        pltpu.make_async_copy(weights[index], columns(index, row), own_sem.at[index]).wait()
    for copy in copies:
        copy.wait()


def exchange(edges, direction, weights, identity):
    whole = pl.BlockSpec(memory_space=pltpu.VMEM)
    shards = len(weights)
    outs = [jax.ShapeDtypeStruct(edge.shape, edge.dtype) for edge in edges]
    outs += [
        jax.ShapeDtypeStruct((part.shape[0], 4 * part.shape[1]), part.dtype) for part in weights
    ]
    return pl.pallas_call(
        functools.partial(halo_kernel, direction, shards),
        out_shape=outs,
        in_specs=[whole] * (3 + shards),
        out_specs=[whole] * (3 + shards),
        scratch_shapes=[
            pltpu.SemaphoreType.DMA((3,)),
            pltpu.SemaphoreType.DMA((3,)),
            pltpu.SemaphoreType.DMA((max(shards, 1),)),
            pltpu.SemaphoreType.DMA((max(shards, 1), 5)),
            pltpu.SemaphoreType.DMA((max(shards, 1), 5)),
        ],
        compiler_params=pltpu.CompilerParams(collective_id=identity, has_side_effects=True),
    )(*edges, *weights)


def lat_swap(value, mask):
    return lax.ppermute(value, "lat", [(index, index ^ mask) for index in range(4)])


def in_owner_order(parts):
    index = lax.axis_index("lat")
    odd, high = index % 2 == 1, index >= 2
    a, b, c, d = parts
    a, b = jnp.where(odd, b, a), jnp.where(odd, a, b)
    c, d = jnp.where(odd, d, c), jnp.where(odd, c, d)
    a, c = jnp.where(high, c, a), jnp.where(high, a, c)
    b, d = jnp.where(high, d, b), jnp.where(high, b, d)
    return jnp.concatenate((a, b, c, d), axis=-1)


def on_device(
    fine_tokens, qkv_weight, proj_weight, merge_one, merge_two, mlp_in, mlp_out, split_weight
):
    levels, rows, cols, width = fine_tokens.shape
    lat_count = lax.axis_size("lat")
    head_dim = width // HEADS
    edges = (
        fine_tokens[:, :SHIFT_R, SHIFT_C:],
        fine_tokens[:, SHIFT_R:, :SHIFT_C],
        fine_tokens[:, :SHIFT_R, :SHIFT_C],
    )
    if lat_count == 4 and lax.axis_size("lon") % 2 == 0:
        row_came, col_came, both_came, full_qkv, full_proj = exchange(
            edges, -1, (qkv_weight, proj_weight), 1
        )
        merge_one, row_came = lax.optimization_barrier((merge_one, row_came))
        merge_far = lat_swap(merge_one, 2)
        merge_parts = (merge_one, lat_swap(merge_one, 1), merge_far, lat_swap(merge_far, 1))
    else:
        row_came, col_came, both_came = exchange(edges, -1, (), 1)
        full_qkv = lax.all_gather(qkv_weight, "lat", axis=1, tiled=True)
        full_proj = lax.all_gather(proj_weight, "lat", axis=1, tiled=True)
    upper = jnp.concatenate([fine_tokens[:, SHIFT_R:, SHIFT_C:], col_came], axis=2)
    lower = jnp.concatenate([row_came, both_came], axis=2)
    moved = jnp.concatenate([upper, lower], axis=1)
    normed = layer_norm(moved.astype(jnp.float32)).astype(jnp.bfloat16).reshape(-1, width)
    qkv = jnp.dot(normed, full_qkv, preferred_element_type=jnp.float32).astype(jnp.bfloat16)
    row_wins = rows // WIN_R
    col_wins = cols // WIN_C
    wins = row_wins * col_wins
    tokens = levels * WIN_R * WIN_C
    parts = qkv.reshape(levels, row_wins, WIN_R, col_wins, WIN_C, 3, HEADS, head_dim)
    parts = parts.transpose(1, 3, 0, 2, 4, 5, 6, 7).reshape(wins, tokens, 3, HEADS, head_dim)
    scores = jnp.einsum(
        "wqhd,wkhd->whqk", parts[:, :, 0], parts[:, :, 1], preferred_element_type=jnp.float32
    )
    scores = scores / math.sqrt(head_dim)
    global_rows = lax.axis_index("lat") * rows + jnp.arange(rows, dtype=jnp.int32)
    wrapped = (global_rows >= rows * lat_count - SHIFT_R).astype(jnp.int32).reshape(row_wins, WIN_R)
    labels = jnp.broadcast_to(
        wrapped[:, None, None, :, None], (row_wins, col_wins, levels, WIN_R, WIN_C)
    )
    labels = labels.reshape(wins, tokens)
    allowed = labels[:, :, None] == labels[:, None, :]
    scores = jnp.where(allowed[:, None], scores, jnp.float32(-1000000000.0))
    top = jnp.max(scores, axis=-1, keepdims=True)
    expo = jnp.exp(scores - top)
    probs = (expo / jnp.sum(expo, axis=-1, keepdims=True)).astype(jnp.bfloat16)
    heads_out = jnp.einsum(
        "whqk,wkhd->wqhd", probs, parts[:, :, 2], preferred_element_type=jnp.float32
    )
    heads_out = heads_out.astype(jnp.bfloat16).reshape(
        row_wins, col_wins, levels, WIN_R, WIN_C, width
    )
    heads_out = heads_out.transpose(2, 0, 3, 1, 4, 5).reshape(-1, width)
    attn = jnp.dot(heads_out, full_proj, preferred_element_type=jnp.float32).astype(jnp.bfloat16)
    attn = attn.reshape(levels, rows, cols, width)
    edges = (
        attn[:, rows - SHIFT_R :, : cols - SHIFT_C],
        attn[:, : rows - SHIFT_R, cols - SHIFT_C :],
        attn[:, rows - SHIFT_R :, cols - SHIFT_C :],
    )
    row_came, col_came, both_came = exchange(edges, 1, (), 2)
    upper = jnp.concatenate([both_came, row_came], axis=2)
    lower = jnp.concatenate([col_came, attn[:, : rows - SHIFT_R, : cols - SHIFT_C]], axis=2)
    back = jnp.concatenate([upper, lower], axis=1)
    fine_out = fine_tokens.astype(jnp.float32) + back.astype(jnp.float32)
    normed1 = layer_norm(cat_four(fine_out)).astype(jnp.bfloat16)
    if lat_count == 4 and lax.axis_size("lon") % 2 == 0:
        merged1 = in_owner_order(
            [
                jnp.dot(normed1, part, preferred_element_type=jnp.float32).astype(jnp.bfloat16)
                for part in merge_parts
            ]
        )
    else:
        merge_all = lax.all_gather(merge_one, "lat", axis=1, tiled=True)
        merged1 = jnp.dot(normed1, merge_all, preferred_element_type=jnp.float32)
        merged1 = merged1.astype(jnp.bfloat16)
    merged1 = merged1.reshape(levels, rows // 2, cols // 2, MID)
    normed2 = layer_norm(cat_four(merged1.astype(jnp.float32))).astype(jnp.bfloat16)
    count = lax.axis_size("lon")
    if count % 2 == 0 and merge_two.shape[1] % (count * 128) == 0:
        blocks = normed2.reshape(normed2.shape[0], count, -1).transpose(1, 0, 2)
        pieces = coarse_in_one(blocks, merge_two, mlp_in, mlp_out, split_weight)
        pieces = pieces.transpose(1, 0, 2)
    else:
        pieces = coarse_apart(normed2, merge_two, mlp_in, mlp_out, split_weight)
    pieces = pieces.reshape(levels, rows // 4, cols // 4, 2, 2, MID).transpose(0, 1, 3, 2, 4, 5)
    pieces = pieces.reshape(levels, rows // 2, cols // 2, MID)
    mid_out = merged1.astype(jnp.float32) + pieces.astype(jnp.float32)
    return (fine_out, mid_out)


def solution(mesh):
    return jax.shard_map(
        on_device,
        mesh=mesh,
        in_specs=(
            P(None, "lat", "lon", None),
            P(None, "lat"),
            P(None, "lat"),
            P(None, "lat"),
            P("lon", None),
            P(None, "lon"),
            P("lon", None),
            P(None, "lon"),
        ),
        out_specs=(P(None, "lat", "lon", None), P(None, "lat", "lon", None)),
        check_vma=False,
    )
```
